128 devices in a mesh: row: 16 (over z_lo, y, core), col: 8 (over x, z_hi).
Axes of the slice: x: 4, y: 4, z: 4 (z_hi: 2, z_lo: 2; z = z_hi * 2 + z_lo), core: 2. Of those that a mesh axis runs over, the one named last changes fastest.
Arguments:
- features: bfloat16 [32768, 128], P(('col', 'row')), may hold values from -6 to 6
- weight: bfloat16 [128, 256], replicated, may hold values from -0.5 to 0.5
- adj_values: bfloat16 [12288, 256, 256], P(('row', 'col')), may hold values from -0.0390625 to 0.0390625
- slot_rows: int32 [12288], P(('row', 'col')), may hold values from 0 to 7, as said below
- slot_cols: int32 [12288], P(('row', 'col')), may hold values from 0 to 15
- slot_live: int32 [128], P(('row', 'col')), may hold values from 13 to 96, as said below
- cotangent: bfloat16 [32768, 256], P(('row', 'col')), may hold values from -6 to 6
Outputs:
- output: bfloat16 [32768, 256], P(('row', 'col'))
- grad_features: bfloat16 [32768, 128], P(('col', 'row'))
- grad_weight: float32 [128, 256], replicated
The draws below stay inside these ranges and needn't reach their ends.
Inputs may be any that keep to these rules, and one draw needn't show every extreme that they name: Within one device's slots the pairs (slot_rows, slot_cols) are distinct. `slot_live`: some device has all 96 slots live.
All inputs are finite; a program needn't handle non-finite values.
Results may differ from the reference program's by a relative error of at most 0.006.
Values may be sent and summed in bfloat16 or wider, within the bound.
A program may use at most 128 MiB of HBM per device.

```python
import math
import jax
import jax.numpy as jnp
from jax import lax

BS = 256
FIN = 128
F = 256
BPD = 1
TILE = 128
SLOTS = 96
NODES = 32768
N_ROW = 16
N_COL = 8


def slot_layout(key):
    keys = jax.random.split(jax.random.fold_in(key, 11), N_ROW * N_COL)
    order = jax.vmap(lambda single: jax.random.permutation(single, TILE))(keys)[:, :SLOTS]
    return order.reshape(-1).astype(jnp.int32)


def draw_slot_rows(key, part):
    return (slot_layout(key) // (BPD * N_ROW)).astype(jnp.int32)


def draw_slot_cols(key, part):
    return (slot_layout(key) % (BPD * N_ROW)).astype(jnp.int32)


def draw_slot_live(key, part):
    counts = jax.random.randint(jax.random.fold_in(key, 23), (N_ROW * N_COL,), SLOTS // 8 + 1, SLOTS + 1)
    fullest = jax.random.randint(jax.random.fold_in(key, 29), (), 0, N_ROW * N_COL)
    return counts.at[fullest].set(SLOTS).astype(jnp.int32)


def block_scale(stream_key, dims, cuts, smallest, high):
    gain = 1.0
    for position, shards_of in cuts:
        draws = jax.random.uniform(jax.random.fold_in(jax.random.fold_in(stream_key, 6), position), (shards_of,), jnp.float32, smallest / len(cuts), high / len(cuts))
        gain = gain * jnp.repeat(jnp.exp(draws), dims[position] // shards_of).reshape((-1,) + (1,) * (len(dims) - 1 - position))
    return gain


def bell_draw(key, extent, spread, reach, cuts=(), kind=jnp.bfloat16):
    drawn = spread * jax.random.normal(key, extent, jnp.float32)
    if cuts:
        drawn = drawn * block_scale(key, extent, cuts, -0.22, 0.18)
    return jnp.clip(drawn, -reach, reach).astype(kind)


def setup_inputs(seed: int = 0) -> dict:
    streams_of = jax.random.split(jax.random.key(seed), 8)
    return {
        "features": bell_draw(streams_of[0], (NODES, FIN), 1.0, 6.0, ((0, 128),)),
        "weight": bell_draw(streams_of[1], (FIN, F), FIN ** -0.5, 0.5),
        "adj_values": bell_draw(streams_of[2], (SLOTS * N_ROW * N_COL, BS, BS), (BS * SLOTS // BPD) ** -0.5, 0.0390625, ((0, 128),)),
        "slot_rows": draw_slot_rows(jax.random.fold_in(streams_of[7], 71), 0),
        "slot_cols": draw_slot_cols(jax.random.fold_in(streams_of[7], 71), 0),
        "slot_live": draw_slot_live(jax.random.fold_in(streams_of[7], 71), 0),
        "cotangent": bell_draw(streams_of[6], (NODES, F), 1.0, 6.0, ((0, 128),)),
    }


def silu_slope(value):
    sig = jax.nn.sigmoid(value)
    return sig * (1.0 + value * (1.0 - sig))

def reference(features, weight, adj_values, slot_rows, slot_cols, slot_live, cotangent):
    tile_rows = BPD * N_COL
    tile_cols = BPD * N_ROW
    blocks = NODES // BS
    projected = jnp.dot(features, weight, preferred_element_type=jnp.float32).astype(jnp.bfloat16)
    source = projected.reshape(blocks, BS, F).astype(jnp.float32)
    positions = jnp.arange(SLOTS, dtype=jnp.int32)
    devices = jnp.arange(N_ROW * N_COL, dtype=jnp.int32)

    def device_terms(device):
        start = (device * SLOTS).astype(jnp.int32)
        values = lax.dynamic_slice_in_dim(adj_values, start, SLOTS, 0).astype(jnp.float32)
        rows = lax.dynamic_slice_in_dim(slot_rows, start, SLOTS, 0) + device // N_COL * tile_rows
        cols = lax.dynamic_slice_in_dim(slot_cols, start, SLOTS, 0) + device % N_COL * tile_cols
        keep = (positions < slot_live[device]).astype(jnp.float32)
        return (values, rows.astype(jnp.int32), cols.astype(jnp.int32), keep)

    def forward_step(total, device):
        values, rows, cols, keep = device_terms(device)
        product = jnp.einsum('sab,sbf->saf', values, source[cols]) * keep[:, None, None]
        return (total.at[rows].add(product), None)
    summed, _ = lax.scan(forward_step, jnp.zeros((blocks, BS, F), jnp.float32), devices)
    summed = summed.reshape(NODES, F)
    output = jax.nn.silu(summed).astype(jnp.bfloat16)
    grad_summed = (cotangent.astype(jnp.float32) * silu_slope(summed)).astype(jnp.bfloat16)
    grad_source = grad_summed.reshape(blocks, BS, F).astype(jnp.float32)

    def backward_step(total, device):
        values, rows, cols, keep = device_terms(device)
        product = jnp.einsum('sab,saf->sbf', values, grad_source[rows]) * keep[:, None, None]
        return (total.at[cols].add(product), None)
    back, _ = lax.scan(backward_step, jnp.zeros((blocks, BS, F), jnp.float32), devices)
    grad_projected = back.reshape(NODES, F).astype(jnp.bfloat16)
    grad_features = jnp.dot(grad_projected, weight.T, preferred_element_type=jnp.float32).astype(jnp.bfloat16)
    grad_weight = jnp.dot(features.T, grad_projected, preferred_element_type=jnp.float32) / math.sqrt(NODES)
    return (output, grad_features, grad_weight)
```

```python
import functools
import math

import jax
import jax.numpy as jnp
from jax import lax
from jax.experimental import pallas as pl
from jax.experimental.pallas import tpu as pltpu
from jax.sharding import PartitionSpec as P

GROUP = 8


def silu_slope(value):
    sig = jax.nn.sigmoid(value)
    return sig * (1.0 + value * (1.0 - sig))


def _block_kernel(transposed, n_in, n_out, rows_ref, cols_ref, live_ref, a_ref, src_ref, out_ref):
    g = pl.program_id(0)
    live = live_ref[0]

    @pl.when(g == 0)
    def _():
        out_ref[...] = jnp.zeros_like(out_ref)

    for k in range(GROUP):
        s = g * GROUP + k

        @pl.when(s < live)
        def _():
            if transposed:
                taken = jnp.clip(rows_ref[s], 0, n_in - 1)
                placed = jnp.clip(cols_ref[s], 0, n_out - 1)
                product = lax.dot_general(
                    a_ref[k], src_ref[taken], (((0,), (0,)), ((), ())),
                    preferred_element_type=jnp.float32,
                )
            else:
                taken = jnp.clip(cols_ref[s], 0, n_in - 1)
                placed = jnp.clip(rows_ref[s], 0, n_out - 1)
                product = jnp.dot(a_ref[k], src_ref[taken], preferred_element_type=jnp.float32)
            out_ref[placed] += product


def block_product(adj_values, slot_rows, slot_cols, slot_live, source, count_out, transposed):
    slots, size, _ = adj_values.shape
    n_in, _, width = source.shape
    steps = slots // GROUP

    def a_map(g, rows, cols, live):
        last = jnp.maximum((live[0] - 1) // GROUP, 0)
        return (jnp.minimum(g, last), 0, 0)

    kernel = functools.partial(_block_kernel, transposed, n_in, count_out)
    return pl.pallas_call(
        kernel,
        grid_spec=pltpu.PrefetchScalarGridSpec(
            num_scalar_prefetch=3,
            grid=(steps,),
            in_specs=[
                pl.BlockSpec((GROUP, size, size), a_map),
                pl.BlockSpec((n_in, size, width), lambda g, r, c, l: (0, 0, 0)),
            ],
            out_specs=pl.BlockSpec((count_out, size, width), lambda g, r, c, l: (0, 0, 0)),
        ),
        out_shape=jax.ShapeDtypeStruct((count_out, size, width), jnp.float32),
        compiler_params=pltpu.CompilerParams(dimension_semantics=("arbitrary",)),
        cost_estimate=pl.CostEstimate(
            flops=2 * slots * size * size * width,
            bytes_accessed=slots * size * size * 2 + n_in * size * width * 2 + count_out * size * width * 4,
            transcendentals=0,
        ),
    )(slot_rows, slot_cols, slot_live, adj_values, source)


def split_dot(left, right, dims):
    high = left.astype(jnp.bfloat16)
    low = (left - high.astype(jnp.float32)).astype(jnp.bfloat16)
    first = lax.dot_general(high, right, dims, preferred_element_type=jnp.float32)
    second = lax.dot_general(low, right, dims, preferred_element_type=jnp.float32)
    return first + second


def body(features, weight, adj_values, slot_rows, slot_cols, slot_live, cotangent):
    size = adj_values.shape[1]
    width = weight.shape[1]
    fin = weight.shape[0]
    own_rows = features.shape[0]
    per_device = own_rows // size
    n_row = lax.axis_size("row")
    n_col = lax.axis_size("col")
    tile_rows = per_device * n_col
    tile_cols = per_device * n_row
    nodes = own_rows * n_row * n_col

    feature_cols = lax.all_gather(features, "row", axis=0, tiled=True)
    projected = jnp.dot(feature_cols, weight, preferred_element_type=jnp.float32).astype(jnp.bfloat16)
    column_blocks = projected.reshape(tile_cols, size, width)
    partial_value = block_product(
        adj_values, slot_rows, slot_cols, slot_live, column_blocks, tile_rows, False
    )
    received = lax.all_to_all(partial_value, "col", 0, 0, tiled=True)
    summed = received.sum(axis=0)
    output = jax.nn.silu(summed).astype(jnp.bfloat16)
    grad_summed = (cotangent.astype(jnp.float32) * silu_slope(summed)).astype(jnp.bfloat16)
    grad_range = lax.all_gather(grad_summed, "col", axis=0, tiled=True)
    grad_blocks = grad_range.reshape(tile_rows, size, width)
    back = block_product(
        adj_values, slot_rows, slot_cols, slot_live, grad_blocks, tile_cols, True
    ).reshape(tile_cols * size, width)
    feature_part = split_dot(back, weight, (((1,), (1,)), ((), ())))
    weight_part = split_dot(back, feature_cols, (((0,), (0,)), ((), ()))).T
    pieces = weight_part.reshape(tile_cols, fin * width // (tile_cols * fin), fin)
    payload = jnp.concatenate([feature_part.reshape(tile_cols, size, fin), pieces], axis=1)
    gathered = lax.all_to_all(payload, "row", 0, 0, tiled=True).sum(axis=0)
    grad_features = gathered[:size].astype(jnp.bfloat16)
    weight_piece = lax.psum(gathered[size:], "col")
    grad_weight = lax.all_gather(weight_piece, "row", axis=0, tiled=True).reshape(fin, width)
    grad_weight = grad_weight / math.sqrt(nodes)
    return (output, grad_features, grad_weight)


def solution(mesh):
    placed = (
        P(("col", "row"), None),
        P(),
        P(("row", "col"), None, None),
        P(("row", "col")),
        P(("row", "col")),
        P(("row", "col")),
        P(("row", "col"), None),
    )
    return jax.shard_map(
        body,
        mesh=mesh,
        in_specs=placed,
        out_specs=(P(("row", "col"), None), P(("col", "row"), None), P()),
        check_vma=False,
    )
```

```python
import functools
import math

import jax
import jax.numpy as jnp
from jax import lax
from jax.experimental import pallas as pl
from jax.experimental.pallas import tpu as pltpu
from jax.sharding import PartitionSpec as P

GROUP = 8


def silu_slope(value):
    sig = jax.nn.sigmoid(value)
    return sig * (1.0 + value * (1.0 - sig))


def _block_kernel(transposed, n_in, n_out, rows_ref, cols_ref, live_ref, a_ref, src_ref, out_ref):
    g = pl.program_id(0)
    live = live_ref[0]

    @pl.when(g == 0)
    def _():
        out_ref[...] = jnp.zeros_like(out_ref)

    @pl.when(g * GROUP < live)
    def _():
        for k in range(GROUP):
            s = g * GROUP + k
            if transposed:
                taken = jnp.clip(rows_ref[s], 0, n_in - 1)
                placed = jnp.clip(cols_ref[s], 0, n_out - 1)
                product = lax.dot_general(
                    a_ref[k], src_ref[taken], (((0,), (0,)), ((), ())),
                    preferred_element_type=jnp.float32,
                )
            else:
                taken = jnp.clip(cols_ref[s], 0, n_in - 1)
                placed = jnp.clip(rows_ref[s], 0, n_out - 1)
                product = jnp.dot(a_ref[k], src_ref[taken], preferred_element_type=jnp.float32)
            keep = jnp.where(s < live, 1.0, 0.0).astype(jnp.float32)
            out_ref[placed] += product * keep


def block_product(adj_values, slot_rows, slot_cols, slot_live, source, count_out, transposed):
    slots, size, _ = adj_values.shape
    n_in, _, width = source.shape
    steps = slots // GROUP

    def a_map(g, rows, cols, live):
        last = jnp.maximum((live[0] - 1) // GROUP, 0)
        return (jnp.minimum(g, last), 0, 0)

    kernel = functools.partial(_block_kernel, transposed, n_in, count_out)
    return pl.pallas_call(
        kernel,
        grid_spec=pltpu.PrefetchScalarGridSpec(
            num_scalar_prefetch=3,
            grid=(steps,),
            in_specs=[
                pl.BlockSpec((GROUP, size, size), a_map),
                pl.BlockSpec((n_in, size, width), lambda g, r, c, l: (0, 0, 0)),
            ],
            out_specs=pl.BlockSpec((count_out, size, width), lambda g, r, c, l: (0, 0, 0)),
        ),
        out_shape=jax.ShapeDtypeStruct((count_out, size, width), jnp.float32),
        compiler_params=pltpu.CompilerParams(dimension_semantics=("arbitrary",)),
        cost_estimate=pl.CostEstimate(
            flops=2 * slots * size * size * width,
            bytes_accessed=slots * size * size * 2 + n_in * size * width * 2 + count_out * size * width * 4,
            transcendentals=0,
        ),
    )(slot_rows, slot_cols, slot_live, adj_values, source)


def gather_axis(block, axis, count):
    spread = jnp.broadcast_to(block[None], (count,) + block.shape)
    return lax.all_to_all(spread, axis, 0, 0, tiled=True)


def split_dot(left, right, dims):
    high = left.astype(jnp.bfloat16)
    low = (left - high.astype(jnp.float32)).astype(jnp.bfloat16)
    first = lax.dot_general(high, right, dims, preferred_element_type=jnp.float32)
    second = lax.dot_general(low, right, dims, preferred_element_type=jnp.float32)
    return first + second


def body(features, weight, adj_values, slot_rows, slot_cols, slot_live, cotangent):
    size = adj_values.shape[1]
    width = weight.shape[1]
    fin = weight.shape[0]
    own_rows = features.shape[0]
    per_device = own_rows // size
    n_row = lax.axis_size("row")
    n_col = lax.axis_size("col")
    tile_rows = per_device * n_col
    tile_cols = per_device * n_row
    nodes = own_rows * n_row * n_col

    feature_cols = gather_axis(features, "row", n_row).reshape(own_rows * n_row, fin)
    projected = jnp.dot(feature_cols, weight, preferred_element_type=jnp.float32).astype(jnp.bfloat16)
    column_blocks = projected.reshape(tile_cols, size, width)
    partial_value = block_product(
        adj_values, slot_rows, slot_cols, slot_live, column_blocks, tile_rows, False
    )
    received = lax.all_to_all(partial_value, "col", 0, 0, tiled=True)
    summed = received.sum(axis=0)
    output = jax.nn.silu(summed).astype(jnp.bfloat16)
    grad_summed = (cotangent.astype(jnp.float32) * silu_slope(summed)).astype(jnp.bfloat16)
    grad_range = gather_axis(grad_summed, "col", n_col)
    grad_blocks = grad_range.reshape(tile_rows, size, width)
    back = block_product(
        adj_values, slot_rows, slot_cols, slot_live, grad_blocks, tile_cols, True
    ).reshape(tile_cols * size, width)
    feature_part = split_dot(back, weight, (((1,), (1,)), ((), ())))
    weight_part = split_dot(back, feature_cols, (((0,), (0,)), ((), ()))).T
    pieces = weight_part.reshape(tile_cols, fin * width // (tile_cols * fin), fin)
    payload = jnp.concatenate([feature_part.reshape(tile_cols, size, fin), pieces], axis=1)
    gathered = lax.all_to_all(payload, "row", 0, 0, tiled=True).sum(axis=0)
    grad_features = gathered[:size].astype(jnp.bfloat16)
    weight_piece = lax.psum(gathered[size:], "col")
    grad_weight = lax.all_gather(weight_piece, "row", axis=0, tiled=True).reshape(fin, width)
    grad_weight = grad_weight / math.sqrt(nodes)
    return (output, grad_features, grad_weight)


def solution(mesh):
    placed = (
        P(("col", "row"), None),
        P(),
        P(("row", "col"), None, None),
        P(("row", "col")),
        P(("row", "col")),
        P(("row", "col")),
        P(("row", "col"), None),
    )
    return jax.shard_map(
        body,
        mesh=mesh,
        in_specs=placed,
        out_specs=(P(("row", "col"), None), P(("col", "row"), None), P()),
        check_vma=False,
    )
```

```python
import functools
import math

import jax
import jax.numpy as jnp
from jax import lax
from jax.experimental import pallas as pl
from jax.experimental.pallas import tpu as pltpu
from jax.sharding import PartitionSpec as P

GROUP = 8


def silu_slope(value):
    sig = jax.nn.sigmoid(value)
    return sig * (1.0 + value * (1.0 - sig))


def _block_kernel(transposed, n_in, n_out, rows_ref, cols_ref, live_ref, a_ref, src_ref, out_ref):
    g = pl.program_id(0)
    live = live_ref[0]

    @pl.when(g == 0)
    def _():
        out_ref[...] = jnp.zeros_like(out_ref)

    @pl.when(g * GROUP < live)
    def _():
        for k in range(GROUP):
            s = g * GROUP + k
            if transposed:
                taken = jnp.clip(rows_ref[s], 0, n_in - 1)
                placed = jnp.clip(cols_ref[s], 0, n_out - 1)
                product = lax.dot_general(
                    a_ref[k], src_ref[taken], (((0,), (0,)), ((), ())),
                    preferred_element_type=jnp.float32,
                )
            else:
                taken = jnp.clip(cols_ref[s], 0, n_in - 1)
                placed = jnp.clip(rows_ref[s], 0, n_out - 1)
                product = jnp.dot(a_ref[k], src_ref[taken], preferred_element_type=jnp.float32)
            keep = jnp.where(s < live, 1.0, 0.0).astype(jnp.float32)
            out_ref[placed] += product * keep


def block_product(adj_values, slot_rows, slot_cols, slot_live, source, count_out, transposed):
    slots, size, _ = adj_values.shape
    n_in, _, width = source.shape
    steps = slots // GROUP

    def a_map(g, rows, cols, live):
        last = jnp.maximum((live[0] - 1) // GROUP, 0)
        return (jnp.minimum(g, last), 0, 0)

    kernel = functools.partial(_block_kernel, transposed, n_in, count_out)
    return pl.pallas_call(
        kernel,
        grid_spec=pltpu.PrefetchScalarGridSpec(
            num_scalar_prefetch=3,
            grid=(steps,),
            in_specs=[
                pl.BlockSpec((GROUP, size, size), a_map),
                pl.BlockSpec((n_in, size, width), lambda g, r, c, l: (0, 0, 0)),
            ],
            out_specs=pl.BlockSpec((count_out, size, width), lambda g, r, c, l: (0, 0, 0)),
        ),
        out_shape=jax.ShapeDtypeStruct((count_out, size, width), jnp.float32),
        compiler_params=pltpu.CompilerParams(dimension_semantics=("arbitrary",)),
        cost_estimate=pl.CostEstimate(
            flops=2 * slots * size * size * width,
            bytes_accessed=slots * size * size * 2 + n_in * size * width * 2 + count_out * size * width * 4,
            transcendentals=0,
        ),
    )(slot_rows, slot_cols, slot_live, adj_values, source)


def gather_axis(block, axis, count):
    spread = jnp.broadcast_to(block[None], (count,) + block.shape)
    return lax.all_to_all(spread, axis, 0, 0, tiled=True)


def split_dot(left, right, dims):
    high = left.astype(jnp.bfloat16)
    low = (left - high.astype(jnp.float32)).astype(jnp.bfloat16)
    first = lax.dot_general(high, right, dims, preferred_element_type=jnp.float32)
    second = lax.dot_general(low, right, dims, preferred_element_type=jnp.float32)
    return first + second


def body(features, weight, adj_values, slot_rows, slot_cols, slot_live, cotangent):
    size = adj_values.shape[1]
    width = weight.shape[1]
    fin = weight.shape[0]
    own_rows = features.shape[0]
    per_device = own_rows // size
    n_row = lax.axis_size("row")
    n_col = lax.axis_size("col")
    tile_rows = per_device * n_col
    tile_cols = per_device * n_row
    nodes = own_rows * n_row * n_col

    feature_cols = gather_axis(features, "row", n_row).reshape(own_rows * n_row, fin)
    projected = jnp.dot(feature_cols, weight, preferred_element_type=jnp.float32).astype(jnp.bfloat16)
    column_blocks = projected.reshape(tile_cols, size, width)
    partial_value = block_product(
        adj_values, slot_rows, slot_cols, slot_live, column_blocks, tile_rows, False
    )
    received = lax.all_to_all(partial_value.astype(jnp.bfloat16), "col", 0, 0, tiled=True)
    summed = received.astype(jnp.float32).sum(axis=0)
    output = jax.nn.silu(summed).astype(jnp.bfloat16)
    grad_summed = (cotangent.astype(jnp.float32) * silu_slope(summed)).astype(jnp.bfloat16)
    grad_range = gather_axis(grad_summed, "col", n_col)
    grad_blocks = grad_range.reshape(tile_rows, size, width)
    back = block_product(
        adj_values, slot_rows, slot_cols, slot_live, grad_blocks, tile_cols, True
    ).reshape(tile_cols * size, width)
    feature_part = split_dot(back, weight, (((1,), (1,)), ((), ())))
    weight_part = split_dot(back, feature_cols, (((0,), (0,)), ((), ()))).T
    pieces = weight_part.reshape(tile_cols, fin * width // (tile_cols * fin), fin)
    payload = jnp.concatenate([feature_part.reshape(tile_cols, size, fin), pieces], axis=1)
    exchanged = lax.all_to_all(payload.astype(jnp.bfloat16), "row", 0, 0, tiled=True)
    gathered = exchanged.astype(jnp.float32).sum(axis=0)
    grad_features = gathered[:size].astype(jnp.bfloat16)
    weight_piece = gather_axis(gathered[size:], "col", n_col).sum(axis=0)
    grad_weight = gather_axis(weight_piece, "row", n_row).reshape(fin, width)
    grad_weight = grad_weight / math.sqrt(nodes)
    return (output, grad_features, grad_weight)


def solution(mesh):
    placed = (
        P(("col", "row"), None),
        P(),
        P(("row", "col"), None, None),
        P(("row", "col")),
        P(("row", "col")),
        P(("row", "col")),
        P(("row", "col"), None),
    )
    return jax.shard_map(
        body,
        mesh=mesh,
        in_specs=placed,
        out_specs=(P(("row", "col"), None), P(("col", "row"), None), P()),
        check_vma=False,
    )
```

```python
import functools
import math

import jax
import jax.numpy as jnp
from jax import lax
from jax.experimental import pallas as pl
from jax.experimental.pallas import tpu as pltpu
from jax.sharding import PartitionSpec as P

GROUP = 8


def silu_slope(value):
    sig = jax.nn.sigmoid(value)
    return sig * (1.0 + value * (1.0 - sig))


def _block_kernel(transposed, n_in, n_out, rows_ref, cols_ref, live_ref, a_ref, src_ref, out_ref):
    g = pl.program_id(0)
    live = live_ref[0]

    @pl.when(g == 0)
    def _():
        out_ref[...] = jnp.zeros_like(out_ref)

    @pl.when(g * GROUP < live)
    def _():
        for k in range(GROUP):
            s = g * GROUP + k
            if transposed:
                taken = jnp.clip(rows_ref[s], 0, n_in - 1)
                placed = jnp.clip(cols_ref[s], 0, n_out - 1)
                product = lax.dot_general(
                    a_ref[k], src_ref[taken], (((0,), (0,)), ((), ())),
                    preferred_element_type=jnp.float32,
                )
            else:
                taken = jnp.clip(cols_ref[s], 0, n_in - 1)
                placed = jnp.clip(rows_ref[s], 0, n_out - 1)
                product = jnp.dot(a_ref[k], src_ref[taken], preferred_element_type=jnp.float32)
            keep = jnp.where(s < live, 1.0, 0.0).astype(jnp.float32)
            out_ref[placed] += product * keep


def block_product(adj_values, slot_rows, slot_cols, slot_live, source, count_out, transposed):
    slots, size, _ = adj_values.shape
    n_in, _, width = source.shape
    steps = slots // GROUP

    def a_map(g, rows, cols, live):
        last = jnp.maximum((live[0] - 1) // GROUP, 0)
        return (jnp.minimum(g, last), 0, 0)

    kernel = functools.partial(_block_kernel, transposed, n_in, count_out)
    return pl.pallas_call(
        kernel,
        grid_spec=pltpu.PrefetchScalarGridSpec(
            num_scalar_prefetch=3,
            grid=(steps,),
            in_specs=[
                pl.BlockSpec((GROUP, size, size), a_map),
                pl.BlockSpec((n_in, size, width), lambda g, r, c, l: (0, 0, 0)),
            ],
            out_specs=pl.BlockSpec((count_out, size, width), lambda g, r, c, l: (0, 0, 0)),
        ),
        out_shape=jax.ShapeDtypeStruct((count_out, size, width), jnp.float32),
        compiler_params=pltpu.CompilerParams(dimension_semantics=("arbitrary",)),
        cost_estimate=pl.CostEstimate(
            flops=2 * slots * size * size * width,
            bytes_accessed=slots * size * size * 2 + n_in * size * width * 2 + count_out * size * width * 4,
            transcendentals=0,
        ),
    )(slot_rows, slot_cols, slot_live, adj_values, source)


def dense_tile(adj_values, slot_rows, slot_cols, slot_live, n_r, n_c):
    slots, size, _ = adj_values.shape
    ids = jnp.arange(slots, dtype=jnp.int32)
    live = ids < slot_live[0]
    flat = jnp.clip(slot_rows, 0, n_r - 1) * n_c + jnp.clip(slot_cols, 0, n_c - 1)
    pos = jnp.full((n_r * n_c,), slots, jnp.int32).at[flat].set(jnp.where(live, ids, slots))
    blocks = jnp.where(
        (pos < slots)[:, None, None], adj_values[jnp.minimum(pos, slots - 1)], jnp.zeros((), adj_values.dtype)
    )
    return blocks.reshape(n_r, n_c, size, size).transpose(0, 2, 1, 3).reshape(n_r * size, n_c * size)


def gather_axis(block, axis, count):
    spread = jnp.broadcast_to(block[None], (count,) + block.shape)
    return lax.all_to_all(spread, axis, 0, 0, tiled=True)


def split_dot(left, right, dims):
    high = left.astype(jnp.bfloat16)
    low = (left - high.astype(jnp.float32)).astype(jnp.bfloat16)
    first = lax.dot_general(high, right, dims, preferred_element_type=jnp.float32)
    second = lax.dot_general(low, right, dims, preferred_element_type=jnp.float32)
    return first + second


def body(features, weight, adj_values, slot_rows, slot_cols, slot_live, cotangent):
    size = adj_values.shape[1]
    width = weight.shape[1]
    fin = weight.shape[0]
    own_rows = features.shape[0]
    per_device = own_rows // size
    n_row = lax.axis_size("row")
    n_col = lax.axis_size("col")
    tile_rows = per_device * n_col
    tile_cols = per_device * n_row
    nodes = own_rows * n_row * n_col

    feature_cols = gather_axis(features, "row", n_row).reshape(own_rows * n_row, fin)
    projected = jnp.dot(feature_cols, weight, preferred_element_type=jnp.float32).astype(jnp.bfloat16)
    matrix = dense_tile(adj_values, slot_rows, slot_cols, slot_live, tile_rows, tile_cols)
    partial_value = jnp.dot(matrix, projected, preferred_element_type=jnp.float32).reshape(tile_rows, size, width)
    received = lax.all_to_all(partial_value.astype(jnp.bfloat16), "col", 0, 0, tiled=True)
    summed = received.astype(jnp.float32).sum(axis=0)
    output = jax.nn.silu(summed).astype(jnp.bfloat16)
    grad_summed = (cotangent.astype(jnp.float32) * silu_slope(summed)).astype(jnp.bfloat16)
    grad_range = gather_axis(grad_summed, "col", n_col)
    back = lax.dot_general(
        matrix, grad_range.reshape(tile_rows * size, width), (((0,), (0,)), ((), ())),
        preferred_element_type=jnp.float32,
    )
    feature_part = split_dot(back, weight, (((1,), (1,)), ((), ())))
    weight_part = split_dot(back, feature_cols, (((0,), (0,)), ((), ()))).T
    pieces = weight_part.reshape(tile_cols, fin * width // (tile_cols * fin), fin)
    payload = jnp.concatenate([feature_part.reshape(tile_cols, size, fin), pieces], axis=1)
    exchanged = lax.all_to_all(payload.astype(jnp.bfloat16), "row", 0, 0, tiled=True)
    gathered = exchanged.astype(jnp.float32).sum(axis=0)
    grad_features = gathered[:size].astype(jnp.bfloat16)
    weight_piece = gather_axis(gathered[size:], "col", n_col).sum(axis=0)
    grad_weight = gather_axis(weight_piece, "row", n_row).reshape(fin, width)
    grad_weight = grad_weight / math.sqrt(nodes)
    return (output, grad_features, grad_weight)


def solution(mesh):
    placed = (
        P(("col", "row"), None),
        P(),
        P(("row", "col"), None, None),
        P(("row", "col")),
        P(("row", "col")),
        P(("row", "col")),
        P(("row", "col"), None),
    )
    return jax.shard_map(
        body,
        mesh=mesh,
        in_specs=placed,
        out_specs=(P(("row", "col"), None), P(("col", "row"), None), P()),
        check_vma=False,
    )
```

```python
import functools
import math

import jax
import jax.numpy as jnp
from jax import lax
from jax.experimental import pallas as pl
from jax.experimental.pallas import tpu as pltpu
from jax.sharding import PartitionSpec as P

GROUP = 8
PARTS = 2


def silu_slope(value):
    sig = jax.nn.sigmoid(value)
    return sig * (1.0 + value * (1.0 - sig))


def _block_kernel(transposed, n_in, n_out, rows_ref, cols_ref, live_ref, a_ref, src_ref, out_ref):
    g = pl.program_id(0)
    live = live_ref[0]

    @pl.when(g == 0)
    def _():
        out_ref[...] = jnp.zeros_like(out_ref)

    @pl.when(g * GROUP < live)
    def _():
        for k in range(GROUP):
            s = g * GROUP + k
            if transposed:
                taken = jnp.clip(rows_ref[s], 0, n_in - 1)
                placed = jnp.clip(cols_ref[s], 0, n_out - 1)
                product = lax.dot_general(
                    a_ref[k], src_ref[taken], (((0,), (0,)), ((), ())),
                    preferred_element_type=jnp.float32,
                )
            else:
                taken = jnp.clip(cols_ref[s], 0, n_in - 1)
                placed = jnp.clip(rows_ref[s], 0, n_out - 1)
                product = jnp.dot(a_ref[k], src_ref[taken], preferred_element_type=jnp.float32)
            keep = jnp.where(s < live, 1.0, 0.0).astype(jnp.float32)
            out_ref[placed] += product * keep


def block_product(adj_values, slot_rows, slot_cols, slot_live, source, count_out, transposed, part=0, parts=1):
    slots, size, _ = adj_values.shape
    n_in, _, full = source.shape
    width = full // parts
    steps = slots // GROUP

    def a_map(g, rows, cols, live):
        last = jnp.maximum((live[0] - 1) // GROUP, 0)
        return (jnp.minimum(g, last), 0, 0)

    kernel = functools.partial(_block_kernel, transposed, n_in, count_out)
    return pl.pallas_call(
        kernel,
        grid_spec=pltpu.PrefetchScalarGridSpec(
            num_scalar_prefetch=3,
            grid=(steps,),
            in_specs=[
                pl.BlockSpec((GROUP, size, size), a_map),
                pl.BlockSpec((n_in, size, width), lambda g, r, c, l: (0, 0, part)),
            ],
            out_specs=pl.BlockSpec((count_out, size, width), lambda g, r, c, l: (0, 0, 0)),
        ),
        out_shape=jax.ShapeDtypeStruct((count_out, size, width), jnp.float32),
        compiler_params=pltpu.CompilerParams(dimension_semantics=("arbitrary",)),
        cost_estimate=pl.CostEstimate(
            flops=2 * slots * size * size * width,
            bytes_accessed=slots * size * size * 2 + n_in * size * width * 2 + count_out * size * width * 4,
            transcendentals=0,
        ),
    )(slot_rows, slot_cols, slot_live, adj_values, source)


def gather_axis(block, axis, count):
    spread = jnp.broadcast_to(block[None], (count,) + block.shape)
    return lax.all_to_all(spread, axis, 0, 0, tiled=True)


def split_dot(left, right, dims):
    high = left.astype(jnp.bfloat16)
    low = (left - high.astype(jnp.float32)).astype(jnp.bfloat16)
    first = lax.dot_general(high, right, dims, preferred_element_type=jnp.float32)
    second = lax.dot_general(low, right, dims, preferred_element_type=jnp.float32)
    return first + second


def body(features, weight, adj_values, slot_rows, slot_cols, slot_live, cotangent):
    size = adj_values.shape[1]
    width = weight.shape[1]
    fin = weight.shape[0]
    own_rows = features.shape[0]
    per_device = own_rows // size
    n_row = lax.axis_size("row")
    n_col = lax.axis_size("col")
    tile_rows = per_device * n_col
    tile_cols = per_device * n_row
    nodes = own_rows * n_row * n_col

    feature_cols = gather_axis(features, "row", n_row).reshape(own_rows * n_row, fin)
    projected = jnp.dot(feature_cols, weight, preferred_element_type=jnp.float32).astype(jnp.bfloat16)
    column_blocks = projected.reshape(tile_cols, size, width)
    outputs, backs = [], []
    for part in range(PARTS):
        partial_value = block_product(
            adj_values, slot_rows, slot_cols, slot_live, column_blocks, tile_rows, False, part, PARTS
        )
        received = lax.all_to_all(partial_value.astype(jnp.bfloat16), "col", 0, 0, tiled=True)
        summed = received.astype(jnp.float32).sum(axis=0)
        outputs.append(jax.nn.silu(summed).astype(jnp.bfloat16))
        cot = cotangent[:, part * (width // PARTS):(part + 1) * (width // PARTS)]
        grad_summed = (cot.astype(jnp.float32) * silu_slope(summed)).astype(jnp.bfloat16)
        grad_range = gather_axis(grad_summed, "col", n_col)
        backs.append(block_product(adj_values, slot_rows, slot_cols, slot_live, grad_range, tile_cols, True))
    output = jnp.concatenate(outputs, axis=1)
    back = jnp.concatenate(backs, axis=2).reshape(tile_cols * size, width)
    feature_part = split_dot(back, weight, (((1,), (1,)), ((), ())))
    weight_part = split_dot(back, feature_cols, (((0,), (0,)), ((), ()))).T
    pieces = weight_part.reshape(tile_cols, fin * width // (tile_cols * fin), fin)
    payload = jnp.concatenate([feature_part.reshape(tile_cols, size, fin), pieces], axis=1)
    exchanged = lax.all_to_all(payload.astype(jnp.bfloat16), "row", 0, 0, tiled=True)
    gathered = exchanged.astype(jnp.float32).sum(axis=0)
    grad_features = gathered[:size].astype(jnp.bfloat16)
    weight_piece = gather_axis(gathered[size:], "col", n_col).sum(axis=0)
    grad_weight = gather_axis(weight_piece, "row", n_row).reshape(fin, width)
    grad_weight = grad_weight / math.sqrt(nodes)
    return (output, grad_features, grad_weight)


def solution(mesh):
    placed = (
        P(("col", "row"), None),
        P(),
        P(("row", "col"), None, None),
        P(("row", "col")),
        P(("row", "col")),
        P(("row", "col")),
        P(("row", "col"), None),
    )
    return jax.shard_map(
        body,
        mesh=mesh,
        in_specs=placed,
        out_specs=(P(("row", "col"), None), P(("col", "row"), None), P()),
        check_vma=False,
    )
```

```python
import functools
import math

import jax
import jax.numpy as jnp
from jax import lax
from jax.experimental import pallas as pl
from jax.experimental.pallas import tpu as pltpu
from jax.sharding import PartitionSpec as P

GROUP = 16


def silu_slope(value):
    sig = jax.nn.sigmoid(value)
    return sig * (1.0 + value * (1.0 - sig))


def _block_kernel(transposed, n_in, n_out, rows_ref, cols_ref, live_ref, a_ref, src_ref, result_ref, out_ref):
    g = pl.program_id(0)
    live = live_ref[0]

    @pl.when(g == 0)
    def _():
        out_ref[...] = jnp.zeros_like(out_ref)

    @pl.when(g * GROUP < live)
    def _():
        for k in range(GROUP):
            s = g * GROUP + k
            if transposed:
                taken = jnp.clip(rows_ref[s], 0, n_in - 1)
                placed = jnp.clip(cols_ref[s], 0, n_out - 1)
                product = lax.dot_general(
                    a_ref[k], src_ref[taken], (((0,), (0,)), ((), ())),
                    preferred_element_type=jnp.float32,
                )
            else:
                taken = jnp.clip(cols_ref[s], 0, n_in - 1)
                placed = jnp.clip(rows_ref[s], 0, n_out - 1)
                product = jnp.dot(a_ref[k], src_ref[taken], preferred_element_type=jnp.float32)
            keep = jnp.where(s < live, 1.0, 0.0).astype(jnp.float32)
            out_ref[placed] += product * keep

    @pl.when(g == pl.num_programs(0) - 1)
    def _():
        result_ref[...] = out_ref[...].astype(result_ref.dtype)


def block_product(adj_values, slot_rows, slot_cols, slot_live, source, count_out, transposed, dtype):
    slots, size, _ = adj_values.shape
    n_in, _, width = source.shape
    steps = slots // GROUP

    def a_map(g, rows, cols, live):
        last = jnp.maximum((live[0] - 1) // GROUP, 0)
        return (jnp.minimum(g, last), 0, 0)

    kernel = functools.partial(_block_kernel, transposed, n_in, count_out)
    return pl.pallas_call(
        kernel,
        grid_spec=pltpu.PrefetchScalarGridSpec(
            num_scalar_prefetch=3,
            grid=(steps,),
            in_specs=[
                pl.BlockSpec((GROUP, size, size), a_map),
                pl.BlockSpec((n_in, size, width), lambda g, r, c, l: (0, 0, 0)),
            ],
            out_specs=pl.BlockSpec((count_out, size, width), lambda g, r, c, l: (0, 0, 0)),
            scratch_shapes=[pltpu.VMEM((count_out, size, width), jnp.float32)],
        ),
        out_shape=jax.ShapeDtypeStruct((count_out, size, width), dtype),
        compiler_params=pltpu.CompilerParams(dimension_semantics=("arbitrary",)),
        cost_estimate=pl.CostEstimate(
            flops=2 * slots * size * size * width,
            bytes_accessed=slots * size * size * 2 + n_in * size * width * 2 + count_out * size * width * 4,
            transcendentals=0,
        ),
    )(slot_rows, slot_cols, slot_live, adj_values, source)


def gather_axis(block, axis, count):
    spread = jnp.broadcast_to(block[None], (count,) + block.shape)
    return lax.all_to_all(spread, axis, 0, 0, tiled=True)


def split_dot(left, right, dims):
    high = left.astype(jnp.bfloat16)
    low = (left - high.astype(jnp.float32)).astype(jnp.bfloat16)
    first = lax.dot_general(high, right, dims, preferred_element_type=jnp.float32)
    second = lax.dot_general(low, right, dims, preferred_element_type=jnp.float32)
    return first + second


def body(features, weight, adj_values, slot_rows, slot_cols, slot_live, cotangent):
    size = adj_values.shape[1]
    width = weight.shape[1]
    fin = weight.shape[0]
    own_rows = features.shape[0]
    per_device = own_rows // size
    n_row = lax.axis_size("row")
    n_col = lax.axis_size("col")
    tile_rows = per_device * n_col
    tile_cols = per_device * n_row
    nodes = own_rows * n_row * n_col

    feature_cols = gather_axis(features, "row", n_row).reshape(own_rows * n_row, fin)
    projected = jnp.dot(feature_cols, weight, preferred_element_type=jnp.float32).astype(jnp.bfloat16)
    column_blocks = projected.reshape(tile_cols, size, width)
    partial_value = block_product(
        adj_values, slot_rows, slot_cols, slot_live, column_blocks, tile_rows, False, jnp.bfloat16
    )
    received = lax.all_to_all(partial_value, "col", 0, 0, tiled=True)
    summed = received.astype(jnp.float32).sum(axis=0)
    output = jax.nn.silu(summed).astype(jnp.bfloat16)
    grad_summed = (cotangent.astype(jnp.float32) * silu_slope(summed)).astype(jnp.bfloat16)
    grad_range = gather_axis(grad_summed, "col", n_col)
    grad_blocks = grad_range.reshape(tile_rows, size, width)
    back = block_product(
        adj_values, slot_rows, slot_cols, slot_live, grad_blocks, tile_cols, True, jnp.float32
    ).reshape(tile_cols * size, width)
    feature_part = split_dot(back, weight, (((1,), (1,)), ((), ())))
    weight_part = split_dot(back, feature_cols, (((0,), (0,)), ((), ()))).T
    pieces = weight_part.reshape(tile_cols, fin * width // (tile_cols * fin), fin)
    payload = jnp.concatenate([feature_part.reshape(tile_cols, size, fin), pieces], axis=1)
    exchanged = lax.all_to_all(payload.astype(jnp.bfloat16), "row", 0, 0, tiled=True)
    gathered = exchanged.astype(jnp.float32).sum(axis=0)
    grad_features = gathered[:size].astype(jnp.bfloat16)
    weight_piece = gather_axis(gathered[size:], "col", n_col).sum(axis=0)
    grad_weight = gather_axis(weight_piece, "row", n_row).reshape(fin, width)
    grad_weight = grad_weight / math.sqrt(nodes)
    return (output, grad_features, grad_weight)


def solution(mesh):
    placed = (
        P(("col", "row"), None),
        P(),
        P(("row", "col"), None, None),
        P(("row", "col")),
        P(("row", "col")),
        P(("row", "col")),
        P(("row", "col"), None),
    )
    return jax.shard_map(
        body,
        mesh=mesh,
        in_specs=placed,
        out_specs=(P(("row", "col"), None), P(("col", "row"), None), P()),
        check_vma=False,
    )
```

```python
import functools
import math

import jax
import jax.numpy as jnp
from jax import lax
from jax.experimental import pallas as pl
from jax.experimental.pallas import tpu as pltpu
from jax.sharding import PartitionSpec as P

GROUP = 32


def silu_slope(value):
    sig = jax.nn.sigmoid(value)
    return sig * (1.0 + value * (1.0 - sig))


def _block_kernel(transposed, n_in, n_out, rows_ref, cols_ref, live_ref, a_ref, src_ref, *refs):
    results, out_ref = refs[:-1], refs[-1]
    g = pl.program_id(0)
    live = live_ref[0]

    @pl.when(g == 0)
    def _():
        out_ref[...] = jnp.zeros_like(out_ref)

    @pl.when(g * GROUP < live)
    def _():
        for k in range(GROUP):
            s = g * GROUP + k
            if transposed:
                taken = jnp.clip(rows_ref[s], 0, n_in - 1)
                placed = jnp.clip(cols_ref[s], 0, n_out - 1)
                product = lax.dot_general(
                    a_ref[k], src_ref[taken], (((0,), (0,)), ((), ())),
                    preferred_element_type=jnp.float32,
                )
            else:
                taken = jnp.clip(cols_ref[s], 0, n_in - 1)
                placed = jnp.clip(rows_ref[s], 0, n_out - 1)
                product = jnp.dot(a_ref[k], src_ref[taken], preferred_element_type=jnp.float32)
            keep = jnp.where(s < live, 1.0, 0.0).astype(jnp.float32)
            out_ref[placed] += product * keep

    @pl.when(g == pl.num_programs(0) - 1)
    def _():
        total = out_ref[...]
        if len(results) == 1:
            results[0][...] = total.astype(results[0].dtype)
        else:
            high = total.astype(jnp.bfloat16)
            results[0][...] = high
            results[1][...] = (total - high.astype(jnp.float32)).astype(jnp.bfloat16)


def block_product(adj_values, slot_rows, slot_cols, slot_live, source, count_out, transposed, dtype, outs=1):
    slots, size, _ = adj_values.shape
    n_in, _, width = source.shape
    steps = slots // GROUP

    def a_map(g, rows, cols, live):
        last = jnp.maximum((live[0] - 1) // GROUP, 0)
        return (jnp.minimum(g, last), 0, 0)

    kernel = functools.partial(_block_kernel, transposed, n_in, count_out)
    return pl.pallas_call(
        kernel,
        grid_spec=pltpu.PrefetchScalarGridSpec(
            num_scalar_prefetch=3,
            grid=(steps,),
            in_specs=[
                pl.BlockSpec((GROUP, size, size), a_map),
                pl.BlockSpec((n_in, size, width), lambda g, r, c, l: (0, 0, 0)),
            ],
            out_specs=[pl.BlockSpec((count_out, size, width), lambda g, r, c, l: (0, 0, 0))] * outs,
            scratch_shapes=[pltpu.VMEM((count_out, size, width), jnp.float32)],
        ),
        out_shape=[jax.ShapeDtypeStruct((count_out, size, width), dtype)] * outs,
        compiler_params=pltpu.CompilerParams(dimension_semantics=("arbitrary",)),
        cost_estimate=pl.CostEstimate(
            flops=2 * slots * size * size * width,
            bytes_accessed=slots * size * size * 2 + n_in * size * width * 2 + count_out * size * width * 4,
            transcendentals=0,
        ),
    )(slot_rows, slot_cols, slot_live, adj_values, source)


def gather_axis(block, axis, count):
    spread = jnp.broadcast_to(block[None], (count,) + block.shape)
    return lax.all_to_all(spread, axis, 0, 0, tiled=True)


def pair_dot(high, low, right, dims):
    first = lax.dot_general(high, right, dims, preferred_element_type=jnp.float32)
    second = lax.dot_general(low, right, dims, preferred_element_type=jnp.float32)
    return first + second


def body(features, weight, adj_values, slot_rows, slot_cols, slot_live, cotangent):
    size = adj_values.shape[1]
    width = weight.shape[1]
    fin = weight.shape[0]
    own_rows = features.shape[0]
    per_device = own_rows // size
    n_row = lax.axis_size("row")
    n_col = lax.axis_size("col")
    tile_rows = per_device * n_col
    tile_cols = per_device * n_row
    nodes = own_rows * n_row * n_col

    feature_cols = gather_axis(features, "row", n_row).reshape(own_rows * n_row, fin)
    projected = jnp.dot(feature_cols, weight, preferred_element_type=jnp.float32).astype(jnp.bfloat16)
    column_blocks = projected.reshape(tile_cols, size, width)
    (partial_value,) = block_product(
        adj_values, slot_rows, slot_cols, slot_live, column_blocks, tile_rows, False, jnp.bfloat16
    )
    received = lax.all_to_all(partial_value, "col", 0, 0, tiled=True)
    summed = received.astype(jnp.float32).sum(axis=0)
    output = jax.nn.silu(summed).astype(jnp.bfloat16)
    grad_summed = (cotangent.astype(jnp.float32) * silu_slope(summed)).astype(jnp.bfloat16)
    grad_range = gather_axis(grad_summed, "col", n_col)
    grad_blocks = grad_range.reshape(tile_rows, size, width)
    back_high, back_low = block_product(
        adj_values, slot_rows, slot_cols, slot_live, grad_blocks, tile_cols, True, jnp.bfloat16, 2
    )
    back_high = back_high.reshape(tile_cols * size, width)
    back_low = back_low.reshape(tile_cols * size, width)
    feature_part = pair_dot(back_high, back_low, weight, (((1,), (1,)), ((), ())))
    weight_part = pair_dot(back_high, back_low, feature_cols, (((0,), (0,)), ((), ()))).T
    pieces = weight_part.reshape(tile_cols, fin * width // (tile_cols * fin), fin)
    payload = jnp.concatenate([feature_part.reshape(tile_cols, size, fin), pieces], axis=1)
    exchanged = lax.all_to_all(payload.astype(jnp.bfloat16), "row", 0, 0, tiled=True)
    gathered = exchanged.astype(jnp.float32).sum(axis=0)
    grad_features = gathered[:size].astype(jnp.bfloat16)
    weight_piece = gather_axis(gathered[size:], "col", n_col).sum(axis=0)
    grad_weight = gather_axis(weight_piece, "row", n_row).reshape(fin, width)
    grad_weight = grad_weight / math.sqrt(nodes)
    return (output, grad_features, grad_weight)


def solution(mesh):
    placed = (
        P(("col", "row"), None),
        P(),
        P(("row", "col"), None, None),
        P(("row", "col")),
        P(("row", "col")),
        P(("row", "col")),
        P(("row", "col"), None),
    )
    return jax.shard_map(
        body,
        mesh=mesh,
        in_specs=placed,
        out_specs=(P(("row", "col"), None), P(("col", "row"), None), P()),
        check_vma=False,
    )
```

```python
import functools
import math

import jax
import jax.numpy as jnp
from jax import lax
from jax.experimental import pallas as pl
from jax.experimental.pallas import tpu as pltpu
from jax.sharding import PartitionSpec as P

GROUP = 32


def silu_slope(value):
    sig = jax.nn.sigmoid(value)
    return sig * (1.0 + value * (1.0 - sig))


def _block_kernel(transposed, n_in, n_out, rows_ref, cols_ref, live_ref, a_ref, src_ref, *refs):
    results, out_ref = refs[:-1], refs[-1]
    g = pl.program_id(0)
    live = live_ref[0]

    @pl.when(g == 0)
    def _():
        out_ref[...] = jnp.zeros_like(out_ref)

    def accumulate(masked):
        for k in range(GROUP):
            s = g * GROUP + k
            if transposed:
                taken = jnp.clip(rows_ref[s], 0, n_in - 1)
                placed = jnp.clip(cols_ref[s], 0, n_out - 1)
                product = lax.dot_general(
                    a_ref[k], src_ref[taken], (((0,), (0,)), ((), ())),
                    preferred_element_type=jnp.float32,
                )
            else:
                taken = jnp.clip(cols_ref[s], 0, n_in - 1)
                placed = jnp.clip(rows_ref[s], 0, n_out - 1)
                product = jnp.dot(a_ref[k], src_ref[taken], preferred_element_type=jnp.float32)
            if masked:
                product = product * jnp.where(s < live, 1.0, 0.0).astype(jnp.float32)
            out_ref[placed] += product

    @pl.when((g + 1) * GROUP <= live)
    def _():
        accumulate(False)

    @pl.when((g * GROUP < live) & ((g + 1) * GROUP > live))
    def _():
        accumulate(True)

    @pl.when(g == pl.num_programs(0) - 1)
    def _():
        total = out_ref[...]
        if len(results) == 1:
            results[0][...] = total.astype(results[0].dtype)
        else:
            high = total.astype(jnp.bfloat16)
            results[0][...] = high
            results[1][...] = (total - high.astype(jnp.float32)).astype(jnp.bfloat16)


def block_product(adj_values, slot_rows, slot_cols, slot_live, source, count_out, transposed, dtype, outs=1):
    slots, size, _ = adj_values.shape
    n_in, _, width = source.shape
    steps = slots // GROUP

    def a_map(g, rows, cols, live):
        last = jnp.maximum((live[0] - 1) // GROUP, 0)
        return (jnp.minimum(g, last), 0, 0)

    kernel = functools.partial(_block_kernel, transposed, n_in, count_out)
    return pl.pallas_call(
        kernel,
        grid_spec=pltpu.PrefetchScalarGridSpec(
            num_scalar_prefetch=3,
            grid=(steps,),
            in_specs=[
                pl.BlockSpec((GROUP, size, size), a_map),
                pl.BlockSpec((n_in, size, width), lambda g, r, c, l: (0, 0, 0)),
            ],
            out_specs=[pl.BlockSpec((count_out, size, width), lambda g, r, c, l: (0, 0, 0))] * outs,
            scratch_shapes=[pltpu.VMEM((count_out, size, width), jnp.float32)],
        ),
        out_shape=[jax.ShapeDtypeStruct((count_out, size, width), dtype)] * outs,
        compiler_params=pltpu.CompilerParams(dimension_semantics=("arbitrary",)),
        cost_estimate=pl.CostEstimate(
            flops=2 * slots * size * size * width,
            bytes_accessed=slots * size * size * 2 + n_in * size * width * 2 + count_out * size * width * 4,
            transcendentals=0,
        ),
    )(slot_rows, slot_cols, slot_live, adj_values, source)


def gather_axis(block, axis, count):
    spread = jnp.broadcast_to(block[None], (count,) + block.shape)
    return lax.all_to_all(spread, axis, 0, 0, tiled=True)


def pair_dot(high, low, right, dims):
    first = lax.dot_general(high, right, dims, preferred_element_type=jnp.float32)
    second = lax.dot_general(low, right, dims, preferred_element_type=jnp.float32)
    return first + second


def body(features, weight, adj_values, slot_rows, slot_cols, slot_live, cotangent):
    size = adj_values.shape[1]
    width = weight.shape[1]
    fin = weight.shape[0]
    own_rows = features.shape[0]
    per_device = own_rows // size
    n_row = lax.axis_size("row")
    n_col = lax.axis_size("col")
    tile_rows = per_device * n_col
    tile_cols = per_device * n_row
    nodes = own_rows * n_row * n_col

    feature_cols = gather_axis(features, "row", n_row).reshape(own_rows * n_row, fin)
    projected = jnp.dot(feature_cols, weight, preferred_element_type=jnp.float32).astype(jnp.bfloat16)
    column_blocks = projected.reshape(tile_cols, size, width)
    (partial_value,) = block_product(
        adj_values, slot_rows, slot_cols, slot_live, column_blocks, tile_rows, False, jnp.bfloat16
    )
    received = lax.all_to_all(partial_value, "col", 0, 0, tiled=True)
    summed = received.astype(jnp.float32).sum(axis=0)
    output = jax.nn.silu(summed).astype(jnp.bfloat16)
    grad_summed = (cotangent.astype(jnp.float32) * silu_slope(summed)).astype(jnp.bfloat16)
    grad_range = gather_axis(grad_summed, "col", n_col)
    grad_blocks = grad_range.reshape(tile_rows, size, width)
    back_high, back_low = block_product(
        adj_values, slot_rows, slot_cols, slot_live, grad_blocks, tile_cols, True, jnp.bfloat16, 2
    )
    back_high = back_high.reshape(tile_cols * size, width)
    back_low = back_low.reshape(tile_cols * size, width)
    feature_part = pair_dot(back_high, back_low, weight, (((1,), (1,)), ((), ())))
    weight_part = pair_dot(back_high, back_low, feature_cols, (((0,), (0,)), ((), ()))).T
    pieces = weight_part.reshape(tile_cols, fin * width // (tile_cols * fin), fin)
    payload = jnp.concatenate([feature_part.reshape(tile_cols, size, fin), pieces], axis=1)
    exchanged = lax.all_to_all(payload.astype(jnp.bfloat16), "row", 0, 0, tiled=True)
    gathered = exchanged.astype(jnp.float32).sum(axis=0)
    grad_features = gathered[:size].astype(jnp.bfloat16)
    weight_piece = gather_axis(gathered[size:], "col", n_col).sum(axis=0)
    grad_weight = gather_axis(weight_piece, "row", n_row).reshape(fin, width)
    grad_weight = grad_weight / math.sqrt(nodes)
    return (output, grad_features, grad_weight)


def solution(mesh):
    placed = (
        P(("col", "row"), None),
        P(),
        P(("row", "col"), None, None),
        P(("row", "col")),
        P(("row", "col")),
        P(("row", "col")),
        P(("row", "col"), None),
    )
    return jax.shard_map(
        body,
        mesh=mesh,
        in_specs=placed,
        out_specs=(P(("row", "col"), None), P(("col", "row"), None), P()),
        check_vma=False,
    )
```

```python
import functools
import math

import jax
import jax.numpy as jnp
from jax import lax
from jax.experimental import pallas as pl
from jax.experimental.pallas import tpu as pltpu
from jax.sharding import PartitionSpec as P

GROUP = 32


def silu_slope(value):
    sig = jax.nn.sigmoid(value)
    return sig * (1.0 + value * (1.0 - sig))


def _block_kernel(transposed, n_in, n_out, project, rows_ref, cols_ref, live_ref, a_ref, *refs):
    if project:
        feat_ref, w_ref = refs[0], refs[1]
        results, out_ref, src_ref = refs[2:-2], refs[-2], refs[-1]
    else:
        src_ref = refs[0]
        results, out_ref = refs[1:-1], refs[-1]
    g = pl.program_id(0)
    live = live_ref[0]

    @pl.when(g == 0)
    def _():
        out_ref[...] = jnp.zeros_like(out_ref)
        if project:
            for c in range(n_in):
                src_ref[c] = jnp.dot(
                    feat_ref[c], w_ref[...], preferred_element_type=jnp.float32
                ).astype(src_ref.dtype)

    def accumulate(masked):
        for k in range(GROUP):
            s = g * GROUP + k
            if transposed:
                taken = jnp.clip(rows_ref[s], 0, n_in - 1)
                placed = jnp.clip(cols_ref[s], 0, n_out - 1)
                product = lax.dot_general(
                    a_ref[k], src_ref[taken], (((0,), (0,)), ((), ())),
                    preferred_element_type=jnp.float32,
                )
            else:
                taken = jnp.clip(cols_ref[s], 0, n_in - 1)
                placed = jnp.clip(rows_ref[s], 0, n_out - 1)
                product = jnp.dot(a_ref[k], src_ref[taken], preferred_element_type=jnp.float32)
            if masked:
                product = product * jnp.where(s < live, 1.0, 0.0).astype(jnp.float32)
            out_ref[placed] += product

    @pl.when((g + 1) * GROUP <= live)
    def _():
        accumulate(False)

    @pl.when((g * GROUP < live) & ((g + 1) * GROUP > live))
    def _():
        accumulate(True)

    @pl.when(g == pl.num_programs(0) - 1)
    def _():
        total = out_ref[...]
        if len(results) == 1:
            results[0][...] = total.astype(results[0].dtype)
        else:
            high = total.astype(jnp.bfloat16)
            results[0][...] = high
            results[1][...] = (total - high.astype(jnp.float32)).astype(jnp.bfloat16)


def block_product(adj_values, slot_rows, slot_cols, slot_live, source, count_out, transposed, dtype, outs=1, weight=None):
    slots, size, _ = adj_values.shape
    project = weight is not None
    n_in = source.shape[0]
    width = weight.shape[1] if project else source.shape[2]
    steps = slots // GROUP
    if project:
        fin = weight.shape[0]
        operands = (source, weight)
        specs = [
            pl.BlockSpec((n_in, size, fin), lambda g, r, c, l: (0, 0, 0)),
            pl.BlockSpec((fin, width), lambda g, r, c, l: (0, 0)),
        ]
        scratch = [pltpu.VMEM((count_out, size, width), jnp.float32), pltpu.VMEM((n_in, size, width), jnp.bfloat16)]
    else:
        operands = (source,)
        specs = [pl.BlockSpec((n_in, size, width), lambda g, r, c, l: (0, 0, 0))]
        scratch = [pltpu.VMEM((count_out, size, width), jnp.float32)]

    def a_map(g, rows, cols, live):
        last = jnp.maximum((live[0] - 1) // GROUP, 0)
        return (jnp.minimum(g, last), 0, 0)

    kernel = functools.partial(_block_kernel, transposed, n_in, count_out, project)
    return pl.pallas_call(
        kernel,
        grid_spec=pltpu.PrefetchScalarGridSpec(
            num_scalar_prefetch=3,
            grid=(steps,),
            in_specs=[pl.BlockSpec((GROUP, size, size), a_map)] + specs,
            out_specs=[pl.BlockSpec((count_out, size, width), lambda g, r, c, l: (0, 0, 0))] * outs,
            scratch_shapes=scratch,
        ),
        out_shape=[jax.ShapeDtypeStruct((count_out, size, width), dtype)] * outs,
        compiler_params=pltpu.CompilerParams(dimension_semantics=("arbitrary",)),
        cost_estimate=pl.CostEstimate(
            flops=2 * slots * size * size * width,
            bytes_accessed=slots * size * size * 2 + n_in * size * width * 2 + count_out * size * width * 4,
            transcendentals=0,
        ),
    )(slot_rows, slot_cols, slot_live, adj_values, *operands)


def gather_axis(block, axis, count):
    spread = jnp.broadcast_to(block[None], (count,) + block.shape)
    return lax.all_to_all(spread, axis, 0, 0, tiled=True)


def pair_dot(high, low, right, dims):
    first = lax.dot_general(high, right, dims, preferred_element_type=jnp.float32)
    second = lax.dot_general(low, right, dims, preferred_element_type=jnp.float32)
    return first + second


def body(features, weight, adj_values, slot_rows, slot_cols, slot_live, cotangent):
    size = adj_values.shape[1]
    width = weight.shape[1]
    fin = weight.shape[0]
    own_rows = features.shape[0]
    per_device = own_rows // size
    n_row = lax.axis_size("row")
    n_col = lax.axis_size("col")
    tile_rows = per_device * n_col
    tile_cols = per_device * n_row
    nodes = own_rows * n_row * n_col

    feature_cols = gather_axis(features, "row", n_row).reshape(own_rows * n_row, fin)
    (partial_value,) = block_product(
        adj_values, slot_rows, slot_cols, slot_live, feature_cols.reshape(tile_cols, size, fin),
        tile_rows, False, jnp.bfloat16, weight=weight,
    )
    received = lax.all_to_all(partial_value, "col", 0, 0, tiled=True)
    summed = received.astype(jnp.float32).sum(axis=0)
    output = jax.nn.silu(summed).astype(jnp.bfloat16)
    grad_summed = (cotangent.astype(jnp.float32) * silu_slope(summed)).astype(jnp.bfloat16)
    grad_range = gather_axis(grad_summed, "col", n_col)
    grad_blocks = grad_range.reshape(tile_rows, size, width)
    back_high, back_low = block_product(
        adj_values, slot_rows, slot_cols, slot_live, grad_blocks, tile_cols, True, jnp.bfloat16, 2
    )
    back_high = back_high.reshape(tile_cols * size, width)
    back_low = back_low.reshape(tile_cols * size, width)
    feature_part = pair_dot(back_high, back_low, weight, (((1,), (1,)), ((), ())))
    weight_part = pair_dot(back_high, back_low, feature_cols, (((0,), (0,)), ((), ()))).T
    pieces = weight_part.reshape(tile_cols, fin * width // (tile_cols * fin), fin)
    payload = jnp.concatenate([feature_part.reshape(tile_cols, size, fin), pieces], axis=1)
    exchanged = lax.all_to_all(payload.astype(jnp.bfloat16), "row", 0, 0, tiled=True)
    gathered = exchanged.astype(jnp.float32).sum(axis=0)
    grad_features = gathered[:size].astype(jnp.bfloat16)
    weight_piece = gather_axis(gathered[size:], "col", n_col).sum(axis=0)
    grad_weight = gather_axis(weight_piece, "row", n_row).reshape(fin, width)
    grad_weight = grad_weight / math.sqrt(nodes)
    return (output, grad_features, grad_weight)


def solution(mesh):
    placed = (
        P(("col", "row"), None),
        P(),
        P(("row", "col"), None, None),
        P(("row", "col")),
        P(("row", "col")),
        P(("row", "col")),
        P(("row", "col"), None),
    )
    return jax.shard_map(
        body,
        mesh=mesh,
        in_specs=placed,
        out_specs=(P(("row", "col"), None), P(("col", "row"), None), P()),
        check_vma=False,
    )
```

```python
import functools
import math

import jax
import jax.numpy as jnp
from jax import lax
from jax.experimental import pallas as pl
from jax.experimental.pallas import tpu as pltpu
from jax.sharding import PartitionSpec as P

GROUP = 32


def silu_slope(value):
    sig = jax.nn.sigmoid(value)
    return sig * (1.0 + value * (1.0 - sig))


def _block_kernel(transposed, n_in, n_out, project, rows_ref, cols_ref, live_ref, a_ref, *refs):
    grads = transposed and len(refs) == 6
    if grads:
        src_ref, feat_ref, w_ref = refs[0], refs[1], refs[2]
        results, out_ref = refs[3:-1], refs[-1]
    elif project:
        feat_ref, w_ref = refs[0], refs[1]
        results, out_ref, src_ref = refs[2:-2], refs[-2], refs[-1]
    else:
        src_ref = refs[0]
        results, out_ref = refs[1:-1], refs[-1]
    g = pl.program_id(0)
    live = live_ref[0]

    @pl.when(g == 0)
    def _():
        out_ref[...] = jnp.zeros_like(out_ref)
        if project:
            for c in range(n_in):
                src_ref[c] = jnp.dot(
                    feat_ref[c], w_ref[...], preferred_element_type=jnp.float32
                ).astype(src_ref.dtype)

    def accumulate(masked):
        for k in range(GROUP):
            s = g * GROUP + k
            if transposed:
                taken = jnp.clip(rows_ref[s], 0, n_in - 1)
                placed = jnp.clip(cols_ref[s], 0, n_out - 1)
                product = lax.dot_general(
                    a_ref[k], src_ref[taken], (((0,), (0,)), ((), ())),
                    preferred_element_type=jnp.float32,
                )
            else:
                taken = jnp.clip(cols_ref[s], 0, n_in - 1)
                placed = jnp.clip(rows_ref[s], 0, n_out - 1)
                product = jnp.dot(a_ref[k], src_ref[taken], preferred_element_type=jnp.float32)
            if masked:
                product = product * jnp.where(s < live, 1.0, 0.0).astype(jnp.float32)
            out_ref[placed] += product

    @pl.when((g + 1) * GROUP <= live)
    def _():
        accumulate(False)

    @pl.when((g * GROUP < live) & ((g + 1) * GROUP > live))
    def _():
        accumulate(True)

    @pl.when(g == pl.num_programs(0) - 1)
    def _():
        if grads:
            dims_f = (((1,), (1,)), ((), ()))
            dims_w = (((0,), (0,)), ((), ()))
            weight_total = jnp.zeros(results[1].shape, jnp.float32)
            for c in range(n_out):
                block = out_ref[c]
                high = block.astype(jnp.bfloat16)
                low = (block - high.astype(jnp.float32)).astype(jnp.bfloat16)
                results[0][c] = lax.dot_general(
                    high, w_ref[...], dims_f, preferred_element_type=jnp.float32
                ) + lax.dot_general(low, w_ref[...], dims_f, preferred_element_type=jnp.float32)
                weight_total = weight_total + lax.dot_general(
                    feat_ref[c], high, dims_w, preferred_element_type=jnp.float32
                ) + lax.dot_general(feat_ref[c], low, dims_w, preferred_element_type=jnp.float32)
            results[1][...] = weight_total
            return
        total = out_ref[...]
        if len(results) == 1:
            results[0][...] = total.astype(results[0].dtype)
        else:
            high = total.astype(jnp.bfloat16)
            results[0][...] = high
            results[1][...] = (total - high.astype(jnp.float32)).astype(jnp.bfloat16)


def block_product(adj_values, slot_rows, slot_cols, slot_live, source, count_out, transposed, dtype, outs=1, weight=None, feats=None):
    slots, size, _ = adj_values.shape
    project = weight is not None and not transposed
    n_in = source.shape[0]
    width = source.shape[2] if transposed or not project else weight.shape[1]
    out_specs = [pl.BlockSpec((count_out, size, width), lambda g, r, c, l: (0, 0, 0))] * outs
    out_shapes = [jax.ShapeDtypeStruct((count_out, size, width), dtype)] * outs
    steps = slots // GROUP
    if transposed and weight is not None:
        fin = weight.shape[0]
        operands = (source, feats, weight)
        specs = [
            pl.BlockSpec((n_in, size, width), lambda g, r, c, l: (0, 0, 0)),
            pl.BlockSpec((count_out, size, fin), lambda g, r, c, l: (0, 0, 0)),
            pl.BlockSpec((fin, width), lambda g, r, c, l: (0, 0)),
        ]
        scratch = [pltpu.VMEM((count_out, size, width), jnp.float32)]
        out_specs = [
            pl.BlockSpec((count_out, size, fin), lambda g, r, c, l: (0, 0, 0)),
            pl.BlockSpec((fin, width), lambda g, r, c, l: (0, 0)),
        ]
        out_shapes = [
            jax.ShapeDtypeStruct((count_out, size, fin), jnp.float32),
            jax.ShapeDtypeStruct((fin, width), jnp.float32),
        ]
    elif project:
        fin = weight.shape[0]
        operands = (source, weight)
        specs = [
            pl.BlockSpec((n_in, size, fin), lambda g, r, c, l: (0, 0, 0)),
            pl.BlockSpec((fin, width), lambda g, r, c, l: (0, 0)),
        ]
        scratch = [pltpu.VMEM((count_out, size, width), jnp.float32), pltpu.VMEM((n_in, size, width), jnp.bfloat16)]
    else:
        operands = (source,)
        specs = [pl.BlockSpec((n_in, size, width), lambda g, r, c, l: (0, 0, 0))]
        scratch = [pltpu.VMEM((count_out, size, width), jnp.float32)]

    def a_map(g, rows, cols, live):
        last = jnp.maximum((live[0] - 1) // GROUP, 0)
        return (jnp.minimum(g, last), 0, 0)

    kernel = functools.partial(_block_kernel, transposed, n_in, count_out, project)
    return pl.pallas_call(
        kernel,
        grid_spec=pltpu.PrefetchScalarGridSpec(
            num_scalar_prefetch=3,
            grid=(steps,),
            in_specs=[pl.BlockSpec((GROUP, size, size), a_map)] + specs,
            out_specs=out_specs,
            scratch_shapes=scratch,
        ),
        out_shape=out_shapes,
        compiler_params=pltpu.CompilerParams(dimension_semantics=("arbitrary",)),
        cost_estimate=pl.CostEstimate(
            flops=2 * slots * size * size * width,
            bytes_accessed=slots * size * size * 2 + n_in * size * width * 2 + count_out * size * width * 4,
            transcendentals=0,
        ),
    )(slot_rows, slot_cols, slot_live, adj_values, *operands)


def gather_axis(block, axis, count):
    spread = jnp.broadcast_to(block[None], (count,) + block.shape)
    return lax.all_to_all(spread, axis, 0, 0, tiled=True)


def pair_dot(high, low, right, dims):
    first = lax.dot_general(high, right, dims, preferred_element_type=jnp.float32)
    second = lax.dot_general(low, right, dims, preferred_element_type=jnp.float32)
    return first + second


def body(features, weight, adj_values, slot_rows, slot_cols, slot_live, cotangent):
    size = adj_values.shape[1]
    width = weight.shape[1]
    fin = weight.shape[0]
    own_rows = features.shape[0]
    per_device = own_rows // size
    n_row = lax.axis_size("row")
    n_col = lax.axis_size("col")
    tile_rows = per_device * n_col
    tile_cols = per_device * n_row
    nodes = own_rows * n_row * n_col

    feature_cols = gather_axis(features, "row", n_row).reshape(own_rows * n_row, fin)
    (partial_value,) = block_product(
        adj_values, slot_rows, slot_cols, slot_live, feature_cols.reshape(tile_cols, size, fin),
        tile_rows, False, jnp.bfloat16, weight=weight,
    )
    received = lax.all_to_all(partial_value, "col", 0, 0, tiled=True)
    summed = received.astype(jnp.float32).sum(axis=0)
    output = jax.nn.silu(summed).astype(jnp.bfloat16)
    grad_summed = (cotangent.astype(jnp.float32) * silu_slope(summed)).astype(jnp.bfloat16)
    grad_range = gather_axis(grad_summed, "col", n_col)
    grad_blocks = grad_range.reshape(tile_rows, size, width)
    feature_part, weight_part = block_product(
        adj_values, slot_rows, slot_cols, slot_live, grad_blocks, tile_cols, True, jnp.float32,
        weight=weight, feats=feature_cols.reshape(tile_cols, size, fin),
    )
    pieces = weight_part.reshape(tile_cols, fin * width // (tile_cols * fin), fin)
    payload = jnp.concatenate([feature_part.reshape(tile_cols, size, fin), pieces], axis=1)
    exchanged = lax.all_to_all(payload.astype(jnp.bfloat16), "row", 0, 0, tiled=True)
    gathered = exchanged.astype(jnp.float32).sum(axis=0)
    grad_features = gathered[:size].astype(jnp.bfloat16)
    weight_piece = gather_axis(gathered[size:], "col", n_col).sum(axis=0)
    grad_weight = gather_axis(weight_piece, "row", n_row).reshape(fin, width)
    grad_weight = grad_weight / math.sqrt(nodes)
    return (output, grad_features, grad_weight)


def solution(mesh):
    placed = (
        P(("col", "row"), None),
        P(),
        P(("row", "col"), None, None),
        P(("row", "col")),
        P(("row", "col")),
        P(("row", "col")),
        P(("row", "col"), None),
    )
    return jax.shard_map(
        body,
        mesh=mesh,
        in_specs=placed,
        out_specs=(P(("row", "col"), None), P(("col", "row"), None), P()),
        check_vma=False,
    )
```

```python
import functools
import math

import jax
import jax.numpy as jnp
from jax import lax
from jax.experimental import pallas as pl
from jax.experimental.pallas import tpu as pltpu
from jax.sharding import PartitionSpec as P

GROUP = 32


def silu_slope(value):
    sig = jax.nn.sigmoid(value)
    return sig * (1.0 + value * (1.0 - sig))


def _block_kernel(transposed, n_in, n_out, project, rows_ref, cols_ref, live_ref, a_ref, *refs):
    grads = transposed and len(refs) == 5
    if grads:
        src_ref, feat_ref, w_ref = refs[0], refs[1], refs[2]
        results, out_ref = refs[3:-1], refs[-1]
    elif project:
        feat_ref, w_ref = refs[0], refs[1]
        results, out_ref, src_ref = refs[2:-2], refs[-2], refs[-1]
    else:
        src_ref = refs[0]
        results, out_ref = refs[1:-1], refs[-1]
    g = pl.program_id(0)
    live = live_ref[0]

    @pl.when(g == 0)
    def _():
        out_ref[...] = jnp.zeros_like(out_ref)
        if project:
            for c in range(n_in):
                src_ref[c] = jnp.dot(
                    feat_ref[c], w_ref[...], preferred_element_type=jnp.float32
                ).astype(src_ref.dtype)

    def accumulate(masked):
        for k in range(GROUP):
            s = g * GROUP + k
            if transposed:
                taken = jnp.clip(rows_ref[s], 0, n_in - 1)
                placed = jnp.clip(cols_ref[s], 0, n_out - 1)
                product = lax.dot_general(
                    a_ref[k], src_ref[taken], (((0,), (0,)), ((), ())),
                    preferred_element_type=jnp.float32,
                )
            else:
                taken = jnp.clip(cols_ref[s], 0, n_in - 1)
                placed = jnp.clip(rows_ref[s], 0, n_out - 1)
                product = jnp.dot(a_ref[k], src_ref[taken], preferred_element_type=jnp.float32)
            if masked:
                product = product * jnp.where(s < live, 1.0, 0.0).astype(jnp.float32)
            out_ref[placed] += product

    @pl.when((g + 1) * GROUP <= live)
    def _():
        accumulate(False)

    @pl.when((g * GROUP < live) & ((g + 1) * GROUP > live))
    def _():
        accumulate(True)

    @pl.when(g == pl.num_programs(0) - 1)
    def _():
        if grads:
            dims_f = (((1,), (1,)), ((), ()))
            dims_w = (((0,), (0,)), ((), ()))
            fin = feat_ref.shape[2]
            size = out_ref.shape[1]
            weight_total = jnp.zeros((fin, out_ref.shape[2]), jnp.float32)
            for c in range(n_out):
                block = out_ref[c]
                high = block.astype(jnp.bfloat16)
                low = (block - high.astype(jnp.float32)).astype(jnp.bfloat16)
                part = lax.dot_general(
                    high, w_ref[...], dims_f, preferred_element_type=jnp.float32
                ) + lax.dot_general(low, w_ref[...], dims_f, preferred_element_type=jnp.float32)
                results[0][c, :size, :] = part.astype(results[0].dtype)
                weight_total = weight_total + lax.dot_general(
                    feat_ref[c], high, dims_w, preferred_element_type=jnp.float32
                ) + lax.dot_general(feat_ref[c], low, dims_w, preferred_element_type=jnp.float32)
            rows_per = fin // n_out
            half = weight_total.shape[1] // 2
            for c in range(n_out):
                chunk = weight_total[c * rows_per:(c + 1) * rows_per]
                results[0][c, size:size + rows_per, :] = chunk[:, :half].astype(results[0].dtype)
                results[0][c, size + rows_per:size + 2 * rows_per, :] = chunk[:, half:].astype(results[0].dtype)
            return
        total = out_ref[...]
        if len(results) == 1:
            results[0][...] = total.astype(results[0].dtype)
        else:
            high = total.astype(jnp.bfloat16)
            results[0][...] = high
            results[1][...] = (total - high.astype(jnp.float32)).astype(jnp.bfloat16)


def block_product(adj_values, slot_rows, slot_cols, slot_live, source, count_out, transposed, dtype, outs=1, weight=None, feats=None):
    slots, size, _ = adj_values.shape
    project = weight is not None and not transposed
    n_in = source.shape[0]
    width = source.shape[2] if transposed or not project else weight.shape[1]
    out_specs = [pl.BlockSpec((count_out, size, width), lambda g, r, c, l: (0, 0, 0))] * outs
    out_shapes = [jax.ShapeDtypeStruct((count_out, size, width), dtype)] * outs
    steps = slots // GROUP
    if transposed and weight is not None:
        fin = weight.shape[0]
        operands = (source, feats, weight)
        specs = [
            pl.BlockSpec((n_in, size, width), lambda g, r, c, l: (0, 0, 0)),
            pl.BlockSpec((count_out, size, fin), lambda g, r, c, l: (0, 0, 0)),
            pl.BlockSpec((fin, width), lambda g, r, c, l: (0, 0)),
        ]
        scratch = [pltpu.VMEM((count_out, size, width), jnp.float32)]
        extra = 2 * (fin // count_out)
        out_specs = [pl.BlockSpec((count_out, size + extra, fin), lambda g, r, c, l: (0, 0, 0))]
        out_shapes = [jax.ShapeDtypeStruct((count_out, size + extra, fin), jnp.bfloat16)]
    elif project:
        fin = weight.shape[0]
        operands = (source, weight)
        specs = [
            pl.BlockSpec((n_in, size, fin), lambda g, r, c, l: (0, 0, 0)),
            pl.BlockSpec((fin, width), lambda g, r, c, l: (0, 0)),
        ]
        scratch = [pltpu.VMEM((count_out, size, width), jnp.float32), pltpu.VMEM((n_in, size, width), jnp.bfloat16)]
    else:
        operands = (source,)
        specs = [pl.BlockSpec((n_in, size, width), lambda g, r, c, l: (0, 0, 0))]
        scratch = [pltpu.VMEM((count_out, size, width), jnp.float32)]

    def a_map(g, rows, cols, live):
        last = jnp.maximum((live[0] - 1) // GROUP, 0)
        return (jnp.minimum(g, last), 0, 0)

    kernel = functools.partial(_block_kernel, transposed, n_in, count_out, project)
    return pl.pallas_call(
        kernel,
        grid_spec=pltpu.PrefetchScalarGridSpec(
            num_scalar_prefetch=3,
            grid=(steps,),
            in_specs=[pl.BlockSpec((GROUP, size, size), a_map)] + specs,
            out_specs=out_specs,
            scratch_shapes=scratch,
        ),
        out_shape=out_shapes,
        compiler_params=pltpu.CompilerParams(dimension_semantics=("arbitrary",)),
        cost_estimate=pl.CostEstimate(
            flops=2 * slots * size * size * width,
            bytes_accessed=slots * size * size * 2 + n_in * size * width * 2 + count_out * size * width * 4,
            transcendentals=0,
        ),
    )(slot_rows, slot_cols, slot_live, adj_values, *operands)


def gather_axis(block, axis, count):
    spread = jnp.broadcast_to(block[None], (count,) + block.shape)
    return lax.all_to_all(spread, axis, 0, 0, tiled=True)


def pair_dot(high, low, right, dims):
    first = lax.dot_general(high, right, dims, preferred_element_type=jnp.float32)
    second = lax.dot_general(low, right, dims, preferred_element_type=jnp.float32)
    return first + second


def body(features, weight, adj_values, slot_rows, slot_cols, slot_live, cotangent):
    size = adj_values.shape[1]
    width = weight.shape[1]
    fin = weight.shape[0]
    own_rows = features.shape[0]
    per_device = own_rows // size
    n_row = lax.axis_size("row")
    n_col = lax.axis_size("col")
    tile_rows = per_device * n_col
    tile_cols = per_device * n_row
    nodes = own_rows * n_row * n_col

    feature_cols = gather_axis(features, "row", n_row).reshape(own_rows * n_row, fin)
    (partial_value,) = block_product(
        adj_values, slot_rows, slot_cols, slot_live, feature_cols.reshape(tile_cols, size, fin),
        tile_rows, False, jnp.bfloat16, weight=weight,
    )
    received = lax.all_to_all(partial_value, "col", 0, 0, tiled=True)
    summed = received.astype(jnp.float32).sum(axis=0)
    output = jax.nn.silu(summed).astype(jnp.bfloat16)
    grad_summed = (cotangent.astype(jnp.float32) * silu_slope(summed)).astype(jnp.bfloat16)
    grad_range = gather_axis(grad_summed, "col", n_col)
    grad_blocks = grad_range.reshape(tile_rows, size, width)
    (payload,) = block_product(
        adj_values, slot_rows, slot_cols, slot_live, grad_blocks, tile_cols, True, jnp.float32,
        weight=weight, feats=feature_cols.reshape(tile_cols, size, fin),
    )
    exchanged = lax.all_to_all(payload, "row", 0, 0, tiled=True)
    gathered = exchanged.astype(jnp.float32).sum(axis=0)
    grad_features = gathered[:size].astype(jnp.bfloat16)
    weight_piece = gather_axis(gathered[size:], "col", n_col).sum(axis=0)
    pieces = gather_axis(weight_piece, "row", n_row)
    rows_per = fin // tile_cols
    grad_weight = pieces.reshape(tile_cols, 2, rows_per, fin).transpose(0, 2, 1, 3).reshape(fin, width)
    grad_weight = grad_weight / math.sqrt(nodes)
    return (output, grad_features, grad_weight)


def solution(mesh):
    placed = (
        P(("col", "row"), None),
        P(),
        P(("row", "col"), None, None),
        P(("row", "col")),
        P(("row", "col")),
        P(("row", "col")),
        P(("row", "col"), None),
    )
    return jax.shard_map(
        body,
        mesh=mesh,
        in_specs=placed,
        out_specs=(P(("row", "col"), None), P(("col", "row"), None), P()),
        check_vma=False,
    )
```

```python
import functools
import math

import jax
import jax.numpy as jnp
from jax import lax
from jax.experimental import pallas as pl
from jax.experimental.pallas import tpu as pltpu
from jax.sharding import PartitionSpec as P

GROUP = 16


def silu_slope(value):
    sig = jax.nn.sigmoid(value)
    return sig * (1.0 + value * (1.0 - sig))


def _block_kernel(transposed, n_in, n_out, project, rows_ref, cols_ref, live_ref, a_ref, *refs):
    grads = transposed and len(refs) == 5
    if grads:
        src_ref, feat_ref, w_ref = refs[0], refs[1], refs[2]
        results, out_ref = refs[3:-1], refs[-1]
    elif project:
        feat_ref, w_ref = refs[0], refs[1]
        results, out_ref, src_ref = refs[2:-2], refs[-2], refs[-1]
    else:
        src_ref = refs[0]
        results, out_ref = refs[1:-1], refs[-1]
    g = pl.program_id(0)
    live = live_ref[0]

    @pl.when(g == 0)
    def _():
        out_ref[...] = jnp.zeros_like(out_ref)
        if project:
            for c in range(n_in):
                src_ref[c] = jnp.dot(
                    feat_ref[c], w_ref[...], preferred_element_type=jnp.float32
                ).astype(src_ref.dtype)

    def accumulate(masked):
        for k in range(GROUP):
            s = g * GROUP + k
            if transposed:
                taken = jnp.clip(rows_ref[s], 0, n_in - 1)
                placed = jnp.clip(cols_ref[s], 0, n_out - 1)
                product = lax.dot_general(
                    a_ref[k], src_ref[taken], (((0,), (0,)), ((), ())),
                    preferred_element_type=jnp.float32,
                )
            else:
                taken = jnp.clip(cols_ref[s], 0, n_in - 1)
                placed = jnp.clip(rows_ref[s], 0, n_out - 1)
                product = jnp.dot(a_ref[k], src_ref[taken], preferred_element_type=jnp.float32)
            if masked:
                product = product * jnp.where(s < live, 1.0, 0.0).astype(jnp.float32)
            out_ref[placed] += product

    @pl.when((g + 1) * GROUP <= live)
    def _():
        accumulate(False)

    @pl.when((g * GROUP < live) & ((g + 1) * GROUP > live))
    def _():
        accumulate(True)

    @pl.when(g == pl.num_programs(0) - 1)
    def _():
        if grads:
            dims_f = (((1,), (1,)), ((), ()))
            dims_w = (((0,), (0,)), ((), ()))
            fin = feat_ref.shape[2]
            size = out_ref.shape[1]
            weight_total = jnp.zeros((fin, out_ref.shape[2]), jnp.float32)
            for c in range(n_out):
                block = out_ref[c]
                high = block.astype(jnp.bfloat16)
                low = (block - high.astype(jnp.float32)).astype(jnp.bfloat16)
                part = lax.dot_general(
                    high, w_ref[...], dims_f, preferred_element_type=jnp.float32
                ) + lax.dot_general(low, w_ref[...], dims_f, preferred_element_type=jnp.float32)
                results[0][c, :size, :] = part.astype(results[0].dtype)
                weight_total = weight_total + lax.dot_general(
                    feat_ref[c], high, dims_w, preferred_element_type=jnp.float32
                ) + lax.dot_general(feat_ref[c], low, dims_w, preferred_element_type=jnp.float32)
            rows_per = fin // n_out
            half = weight_total.shape[1] // 2
            for c in range(n_out):
                chunk = weight_total[c * rows_per:(c + 1) * rows_per]
                results[0][c, size:size + rows_per, :] = chunk[:, :half].astype(results[0].dtype)
                results[0][c, size + rows_per:size + 2 * rows_per, :] = chunk[:, half:].astype(results[0].dtype)
            return
        total = out_ref[...]
        if len(results) == 1:
            results[0][...] = total.astype(results[0].dtype)
        else:
            high = total.astype(jnp.bfloat16)
            results[0][...] = high
            results[1][...] = (total - high.astype(jnp.float32)).astype(jnp.bfloat16)


def block_product(adj_values, slot_rows, slot_cols, slot_live, source, count_out, transposed, dtype, outs=1, weight=None, feats=None):
    slots, size, _ = adj_values.shape
    project = weight is not None and not transposed
    n_in = source.shape[0]
    width = source.shape[2] if transposed or not project else weight.shape[1]
    out_specs = [pl.BlockSpec((count_out, size, width), lambda g, r, c, l: (0, 0, 0))] * outs
    out_shapes = [jax.ShapeDtypeStruct((count_out, size, width), dtype)] * outs
    steps = slots // GROUP
    if transposed and weight is not None:
        fin = weight.shape[0]
        operands = (source, feats, weight)
        specs = [
            pl.BlockSpec((n_in, size, width), lambda g, r, c, l: (0, 0, 0)),
            pl.BlockSpec((count_out, size, fin), lambda g, r, c, l: (0, 0, 0)),
            pl.BlockSpec((fin, width), lambda g, r, c, l: (0, 0)),
        ]
        scratch = [pltpu.VMEM((count_out, size, width), jnp.float32)]
        extra = 2 * (fin // count_out)
        out_specs = [pl.BlockSpec((count_out, size + extra, fin), lambda g, r, c, l: (0, 0, 0))]
        out_shapes = [jax.ShapeDtypeStruct((count_out, size + extra, fin), jnp.bfloat16)]
    elif project:
        fin = weight.shape[0]
        operands = (source, weight)
        specs = [
            pl.BlockSpec((n_in, size, fin), lambda g, r, c, l: (0, 0, 0)),
            pl.BlockSpec((fin, width), lambda g, r, c, l: (0, 0)),
        ]
        scratch = [pltpu.VMEM((count_out, size, width), jnp.float32), pltpu.VMEM((n_in, size, width), jnp.bfloat16)]
    else:
        operands = (source,)
        specs = [pl.BlockSpec((n_in, size, width), lambda g, r, c, l: (0, 0, 0))]
        scratch = [pltpu.VMEM((count_out, size, width), jnp.float32)]

    def a_map(g, rows, cols, live):
        last = jnp.maximum((live[0] - 1) // GROUP, 0)
        return (jnp.minimum(g, last), 0, 0)

    kernel = functools.partial(_block_kernel, transposed, n_in, count_out, project)
    return pl.pallas_call(
        kernel,
        grid_spec=pltpu.PrefetchScalarGridSpec(
            num_scalar_prefetch=3,
            grid=(steps,),
            in_specs=[pl.BlockSpec((GROUP, size, size), a_map)] + specs,
            out_specs=out_specs,
            scratch_shapes=scratch,
        ),
        out_shape=out_shapes,
        compiler_params=pltpu.CompilerParams(dimension_semantics=("arbitrary",)),
        cost_estimate=pl.CostEstimate(
            flops=2 * slots * size * size * width,
            bytes_accessed=slots * size * size * 2 + n_in * size * width * 2 + count_out * size * width * 4,
            transcendentals=0,
        ),
    )(slot_rows, slot_cols, slot_live, adj_values, *operands)


def gather_axis(block, axis, count):
    spread = jnp.broadcast_to(block[None], (count,) + block.shape)
    return lax.all_to_all(spread, axis, 0, 0, tiled=True)


def pair_dot(high, low, right, dims):
    first = lax.dot_general(high, right, dims, preferred_element_type=jnp.float32)
    second = lax.dot_general(low, right, dims, preferred_element_type=jnp.float32)
    return first + second


def body(features, weight, adj_values, slot_rows, slot_cols, slot_live, cotangent):
    size = adj_values.shape[1]
    width = weight.shape[1]
    fin = weight.shape[0]
    own_rows = features.shape[0]
    per_device = own_rows // size
    n_row = lax.axis_size("row")
    n_col = lax.axis_size("col")
    tile_rows = per_device * n_col
    tile_cols = per_device * n_row
    nodes = own_rows * n_row * n_col

    feature_cols = gather_axis(features, "row", n_row).reshape(own_rows * n_row, fin)
    (partial_value,) = block_product(
        adj_values, slot_rows, slot_cols, slot_live, feature_cols.reshape(tile_cols, size, fin),
        tile_rows, False, jnp.bfloat16, weight=weight,
    )
    received = lax.all_to_all(partial_value, "col", 0, 0, tiled=True)
    summed = received.astype(jnp.float32).sum(axis=0)
    output = jax.nn.silu(summed).astype(jnp.bfloat16)
    grad_summed = (cotangent.astype(jnp.float32) * silu_slope(summed)).astype(jnp.bfloat16)
    grad_range = gather_axis(grad_summed, "col", n_col)
    grad_blocks = grad_range.reshape(tile_rows, size, width)
    (payload,) = block_product(
        adj_values, slot_rows, slot_cols, slot_live, grad_blocks, tile_cols, True, jnp.float32,
        weight=weight, feats=feature_cols.reshape(tile_cols, size, fin),
    )
    exchanged = lax.all_to_all(payload, "row", 0, 0, tiled=True)
    gathered = exchanged.astype(jnp.float32).sum(axis=0)
    grad_features = gathered[:size].astype(jnp.bfloat16)
    weight_piece = gather_axis(gathered[size:], "col", n_col).sum(axis=0)
    pieces = gather_axis(weight_piece, "row", n_row)
    rows_per = fin // tile_cols
    grad_weight = pieces.reshape(tile_cols, 2, rows_per, fin).transpose(0, 2, 1, 3).reshape(fin, width)
    grad_weight = grad_weight / math.sqrt(nodes)
    return (output, grad_features, grad_weight)


def solution(mesh):
    placed = (
        P(("col", "row"), None),
        P(),
        P(("row", "col"), None, None),
        P(("row", "col")),
        P(("row", "col")),
        P(("row", "col")),
        P(("row", "col"), None),
    )
    return jax.shard_map(
        body,
        mesh=mesh,
        in_specs=placed,
        out_specs=(P(("row", "col"), None), P(("col", "row"), None), P()),
        check_vma=False,
    )
```

```python
import functools
import math

import jax
import jax.numpy as jnp
from jax import lax
from jax.experimental import pallas as pl
from jax.experimental.pallas import tpu as pltpu
from jax.sharding import PartitionSpec as P

GROUP = 32


def silu_slope(value):
    sig = jax.nn.sigmoid(value)
    return sig * (1.0 + value * (1.0 - sig))


def _block_kernel(transposed, n_in, n_out, project, rows_ref, cols_ref, live_ref, a_ref, *refs):
    grads = transposed and len(refs) == 5
    if grads:
        src_ref, feat_ref, w_ref = refs[0], refs[1], refs[2]
        results, out_ref = refs[3:-1], refs[-1]
    elif project:
        feat_ref, w_ref = refs[0], refs[1]
        results, out_ref, src_ref = refs[2:-2], refs[-2], refs[-1]
    else:
        src_ref = refs[0]
        results, out_ref = refs[1:-1], refs[-1]
    g = pl.program_id(0)
    live = live_ref[0]

    @pl.when(g == 0)
    def _():
        out_ref[...] = jnp.zeros_like(out_ref)
        if project:
            for c in range(n_in):
                src_ref[c] = jnp.dot(
                    feat_ref[c], w_ref[...], preferred_element_type=jnp.float32
                ).astype(src_ref.dtype)

    def accumulate(masked):
        for k in range(GROUP):
            s = g * GROUP + k
            if transposed:
                taken = jnp.clip(rows_ref[s], 0, n_in - 1)
                placed = jnp.clip(cols_ref[s], 0, n_out - 1)
                product = lax.dot_general(
                    a_ref[k], src_ref[taken], (((0,), (0,)), ((), ())),
                    preferred_element_type=jnp.float32,
                )
            else:
                taken = jnp.clip(cols_ref[s], 0, n_in - 1)
                placed = jnp.clip(rows_ref[s], 0, n_out - 1)
                product = jnp.dot(a_ref[k], src_ref[taken], preferred_element_type=jnp.float32)
            if masked:
                product = product * jnp.where(s < live, 1.0, 0.0).astype(jnp.float32)
            out_ref[placed] += product

    @pl.when((g + 1) * GROUP <= live)
    def _():
        accumulate(False)

    @pl.when((g * GROUP < live) & ((g + 1) * GROUP > live))
    def _():
        accumulate(True)

    @pl.when(g == pl.num_programs(0) - 1)
    def _():
        if grads:
            dims_f = (((1,), (1,)), ((), ()))
            dims_w = (((0,), (0,)), ((), ()))
            fin = feat_ref.shape[2]
            size = out_ref.shape[1]
            weight_total = jnp.zeros((fin, out_ref.shape[2]), jnp.float32)
            for c in range(n_out):
                block = out_ref[c]
                high = block.astype(jnp.bfloat16)
                low = (block - high.astype(jnp.float32)).astype(jnp.bfloat16)
                part = lax.dot_general(
                    high, w_ref[...], dims_f, preferred_element_type=jnp.float32
                ) + lax.dot_general(low, w_ref[...], dims_f, preferred_element_type=jnp.float32)
                results[0][c, :size, :] = part.astype(results[0].dtype)
                weight_total = weight_total + lax.dot_general(
                    feat_ref[c], high, dims_w, preferred_element_type=jnp.float32
                ) + lax.dot_general(feat_ref[c], low, dims_w, preferred_element_type=jnp.float32)
            rows_per = fin // n_out
            half = weight_total.shape[1] // 2
            for c in range(n_out):
                chunk = weight_total[c * rows_per:(c + 1) * rows_per]
                results[0][c, size:size + rows_per, :] = chunk[:, :half].astype(results[0].dtype)
                results[0][c, size + rows_per:size + 2 * rows_per, :] = chunk[:, half:].astype(results[0].dtype)
            return
        total = out_ref[...]
        if len(results) == 1:
            results[0][...] = total.astype(results[0].dtype)
        else:
            high = total.astype(jnp.bfloat16)
            results[0][...] = high
            results[1][...] = (total - high.astype(jnp.float32)).astype(jnp.bfloat16)


def block_product(adj_values, slot_rows, slot_cols, slot_live, source, count_out, transposed, dtype, outs=1, weight=None, feats=None):
    slots, size, _ = adj_values.shape
    project = weight is not None and not transposed
    n_in = source.shape[0]
    width = source.shape[2] if transposed or not project else weight.shape[1]
    out_specs = [pl.BlockSpec((count_out, size, width), lambda g, r, c, l: (0, 0, 0))] * outs
    out_shapes = [jax.ShapeDtypeStruct((count_out, size, width), dtype)] * outs
    steps = slots // GROUP
    if transposed and weight is not None:
        fin = weight.shape[0]
        operands = (source, feats, weight)
        specs = [
            pl.BlockSpec((n_in, size, width), lambda g, r, c, l: (0, 0, 0)),
            pl.BlockSpec((count_out, size, fin), lambda g, r, c, l: (0, 0, 0)),
            pl.BlockSpec((fin, width), lambda g, r, c, l: (0, 0)),
        ]
        scratch = [pltpu.VMEM((count_out, size, width), jnp.float32)]
        extra = 2 * (fin // count_out)
        out_specs = [pl.BlockSpec((count_out, size + extra, fin), lambda g, r, c, l: (0, 0, 0))]
        out_shapes = [jax.ShapeDtypeStruct((count_out, size + extra, fin), jnp.bfloat16)]
    elif project:
        fin = weight.shape[0]
        operands = (source, weight)
        specs = [
            pl.BlockSpec((n_in, size, fin), lambda g, r, c, l: (0, 0, 0)),
            pl.BlockSpec((fin, width), lambda g, r, c, l: (0, 0)),
        ]
        scratch = [pltpu.VMEM((count_out, size, width), jnp.float32), pltpu.VMEM((n_in, size, width), jnp.bfloat16)]
    else:
        operands = (source,)
        specs = [pl.BlockSpec((n_in, size, width), lambda g, r, c, l: (0, 0, 0))]
        scratch = [pltpu.VMEM((count_out, size, width), jnp.float32)]

    def a_map(g, rows, cols, live):
        last = jnp.maximum((live[0] - 1) // GROUP, 0)
        return (jnp.minimum(g, last), 0, 0)

    kernel = functools.partial(_block_kernel, transposed, n_in, count_out, project)
    return pl.pallas_call(
        kernel,
        grid_spec=pltpu.PrefetchScalarGridSpec(
            num_scalar_prefetch=3,
            grid=(steps,),
            in_specs=[pl.BlockSpec((GROUP, size, size), a_map)] + specs,
            out_specs=out_specs,
            scratch_shapes=scratch,
        ),
        out_shape=out_shapes,
        compiler_params=pltpu.CompilerParams(dimension_semantics=("arbitrary",)),
        cost_estimate=pl.CostEstimate(
            flops=2 * slots * size * size * width,
            bytes_accessed=slots * size * size * 2 + n_in * size * width * 2 + count_out * size * width * 4,
            transcendentals=0,
        ),
    )(slot_rows, slot_cols, slot_live, adj_values, *operands)


def gather_axis(block, axis, count):
    spread = jnp.broadcast_to(block[None], (count,) + block.shape)
    return lax.all_to_all(spread, axis, 0, 0, tiled=True)


def pair_dot(high, low, right, dims):
    first = lax.dot_general(high, right, dims, preferred_element_type=jnp.float32)
    second = lax.dot_general(low, right, dims, preferred_element_type=jnp.float32)
    return first + second


def body(features, weight, adj_values, slot_rows, slot_cols, slot_live, cotangent):
    size = adj_values.shape[1]
    width = weight.shape[1]
    fin = weight.shape[0]
    own_rows = features.shape[0]
    per_device = own_rows // size
    n_row = lax.axis_size("row")
    n_col = lax.axis_size("col")
    tile_rows = per_device * n_col
    tile_cols = per_device * n_row
    nodes = own_rows * n_row * n_col

    feature_cols = gather_axis(features, "row", n_row).reshape(own_rows * n_row, fin)
    (partial_value,) = block_product(
        adj_values, slot_rows, slot_cols, slot_live, feature_cols.reshape(tile_cols, size, fin),
        tile_rows, False, jnp.bfloat16, weight=weight,
    )
    received = lax.all_to_all(partial_value, "col", 0, 0, tiled=True)
    summed = received.astype(jnp.float32).sum(axis=0)
    output = jax.nn.silu(summed).astype(jnp.bfloat16)
    grad_summed = (cotangent.astype(jnp.float32) * silu_slope(summed)).astype(jnp.bfloat16)
    grad_range = gather_axis(grad_summed, "col", n_col)
    grad_blocks = grad_range.reshape(tile_rows, size, width)
    (payload,) = block_product(
        adj_values, slot_rows, slot_cols, slot_live, grad_blocks, tile_cols, True, jnp.float32,
        weight=weight, feats=feature_cols.reshape(tile_cols, size, fin),
    )
    exchanged = lax.all_to_all(payload, "row", 0, 0, tiled=True)
    weight_in = exchanged[:, size:].astype(jnp.float32).sum(axis=0)
    grad_features = exchanged[:, :size].astype(jnp.float32).sum(axis=0).astype(jnp.bfloat16)
    weight_piece = gather_axis(weight_in, "col", n_col).sum(axis=0)
    pieces = gather_axis(weight_piece, "row", n_row)
    rows_per = fin // tile_cols
    grad_weight = pieces.reshape(tile_cols, 2, rows_per, fin).transpose(0, 2, 1, 3).reshape(fin, width)
    grad_weight = grad_weight / math.sqrt(nodes)
    return (output, grad_features, grad_weight)


def solution(mesh):
    placed = (
        P(("col", "row"), None),
        P(),
        P(("row", "col"), None, None),
        P(("row", "col")),
        P(("row", "col")),
        P(("row", "col")),
        P(("row", "col"), None),
    )
    return jax.shard_map(
        body,
        mesh=mesh,
        in_specs=placed,
        out_specs=(P(("row", "col"), None), P(("col", "row"), None), P()),
        check_vma=False,
    )
```
